256 devices in a mesh: fsdp: 4 (over x), seq: 64 (over z, y, core).
Axes of the slice: x: 4, y: 4, z: 8, core: 2. Of those that a mesh axis runs over, the one named last changes fastest.
Arguments:
- tokens: bfloat16 [4, 16384, 4096], P('fsdp', 'seq'), may hold values from -6 to 6
- queries: bfloat16 [4, 16384, 4096], P('fsdp', 'seq'), may hold values from -70 to 70
- key_weight: bfloat16 [4096, 1024], P(('fsdp', 'seq')), may hold values from -0.09375 to 0.09375
- value_weight: bfloat16 [4096, 1024], P(('fsdp', 'seq')), may hold values from -0.09375 to 0.09375
- sorted_blocks: int32 [4, 8, 128], P('fsdp', None, 'seq'), may hold values from 0 to 127, as said below
Outputs:
- attended: bfloat16 [4, 16384, 4096], P('fsdp', 'seq')
The draws below stay inside these ranges and needn't reach their ends.
Inputs may be any that keep to these rules, and one draw needn't show every extreme that they name: `sorted_blocks`: for each sequence and key-value head, a permutation of the 128 blocks. The 2 blocks of one device, over all key-value heads, name blocks that lie on one device at most 1 times, and for one head at most 1 times; both bounds are reached in every draw. Device d holds blocks d * 2 to d * 2 + 1.
All inputs are finite; a program needn't handle non-finite values.
Results may differ from the reference program's by a relative error of at most 0.012.
The reference program's roundings to bfloat16 on the way count: a program that leaves them out, or rounds other values in their place, can miss the bound.
Values may be sent and summed in bfloat16 or wider, within the bound.
A program may use at most 128 MiB of HBM per device.

```python
import math
import jax
import jax.numpy as jnp
from jax import lax

D = 4096
DH = 128
KVH = 8
GROUP = 4
BLOCK = 128
BLK_DEV = 2
NB = 128
L = 16384
SEQS = 4


def draw_queries(key, part):
    first_key = jax.random.fold_in(jax.random.fold_in(key, 11), 0)
    values_out = jnp.clip(jax.random.normal(first_key, (SEQS, L, KVH * GROUP * DH), jnp.float32), -6.0, 6.0)
    return values_out.astype(jnp.bfloat16)


def one_sequence(seq_key):
    devices = NB // BLK_DEV
    first_key, second_key, third_key = jax.random.split(seq_key, 3)
    relabel = jax.random.permutation(first_key, devices)
    inverse = jnp.argsort(relabel)
    shifts = jax.random.permutation(second_key, devices)[jnp.arange(KVH * BLK_DEV) % devices].reshape(KVH, BLK_DEV)
    slot_perm = jax.vmap(lambda slot_key: jax.random.permutation(slot_key, BLK_DEV))(jax.random.split(third_key, KVH))
    target = relabel[(inverse[None, :, None] + shifts[:, None, :]) % devices]
    return (target * BLK_DEV + slot_perm[:, None, :]).reshape(KVH, NB).astype(jnp.int32)


def draw_sorted_blocks(key, part):
    base_key = jax.random.fold_in(key, 23)
    seq_keys = jax.vmap(lambda index: jax.random.fold_in(base_key, index))(jnp.arange(SEQS))
    return jax.vmap(one_sequence)(seq_keys)


def block_levels(key, shape, shards, least, top_value):
    gain = 1.0
    for position, parts in shards:
        heights = jax.random.uniform(jax.random.fold_in(jax.random.fold_in(key, 6), position), (parts,), jnp.float32, least / len(shards), top_value / len(shards))
        gain = gain * jnp.repeat(jnp.exp(heights), shape[position] // parts).reshape((-1,) + (1,) * (len(shape) - 1 - position))
    return gain


def gaussian(own_key, dims, deviation, reach, pieces=(), kind=jnp.bfloat16):
    drawn = jax.random.normal(own_key, dims, jnp.float32) * deviation
    if len(pieces) > 0:
        drawn = block_levels(own_key, dims, pieces, -0.22, 0.18) * drawn
    return jnp.clip(drawn, min=-reach, max=reach).astype(kind)


def setup_inputs(seed: int = 0) -> dict:
    streams_of = jax.random.split(jax.random.key(seed), 6)
    return {
        "tokens": gaussian(streams_of[0], (SEQS, L, D), 1.0, 6.0, ((0, 4), (1, 64))),
        "queries": draw_queries(jax.random.fold_in(streams_of[5], 71), 0),
        "key_weight": gaussian(streams_of[2], (D, KVH * DH), D ** -0.5, 0.09375, ((0, 256),)),
        "value_weight": gaussian(streams_of[3], (D, KVH * DH), D ** -0.5, 0.09375, ((0, 256),)),
        "sorted_blocks": draw_sorted_blocks(jax.random.fold_in(streams_of[5], 71), 0),
    }


def attend_head(query_head, candidate_head):
    key_part = candidate_head[:, :, :DH].astype(jnp.float32)
    value_part = candidate_head[:, :, DH:].astype(jnp.float32)
    scores = jnp.einsum('btge,bke->gbtk', query_head.astype(jnp.float32), key_part) * (1.0 / math.sqrt(DH))
    block_index = jnp.arange(NB, dtype=jnp.int32)
    key_index = jnp.arange(3 * BLOCK, dtype=jnp.int32)
    blocked = (block_index[:, None] == 0) & (key_index[None, :] >= BLOCK) & (key_index[None, :] < 2 * BLOCK)
    scores = jnp.where(blocked[None, :, None, :], -1e+30, scores)
    highest = lax.optimization_barrier(jnp.max(scores, axis=-1, keepdims=True))
    raised = jnp.exp(scores - highest)
    weights = (raised / lax.optimization_barrier(jnp.sum(raised, axis=-1, keepdims=True))).astype(jnp.bfloat16)
    result = jnp.einsum('gbtk,bke->btge', weights.astype(jnp.float32), value_part)
    return result.astype(jnp.bfloat16)

def pick_blocks(kv_table, wanted):
    return jnp.take(kv_table, wanted, axis=0)

def run_head(inputs):
    return attend_head(inputs[0], inputs[1])

def reference(tokens, queries, key_weight, value_weight, sorted_blocks):
    outputs = []
    for sequence in range(SEQS):
        key_all = jnp.dot(tokens[sequence], key_weight, preferred_element_type=jnp.float32).astype(jnp.bfloat16)
        value_all = jnp.dot(tokens[sequence], value_weight, preferred_element_type=jnp.float32).astype(jnp.bfloat16)
        key_blocks = key_all.reshape(NB, BLOCK, KVH, DH)
        value_blocks = value_all.reshape(NB, BLOCK, KVH, DH)
        packed = jnp.concatenate([key_blocks, value_blocks], axis=3).transpose(2, 0, 1, 3)
        preceding = jnp.concatenate([jnp.zeros_like(packed[:, :1]), packed[:, :NB - 1]], axis=1)
        chosen = jax.vmap(pick_blocks)(packed, sorted_blocks[sequence].astype(jnp.int32))
        candidates = jnp.concatenate([packed, preceding, chosen], axis=2)
        query_heads = queries[sequence].reshape(NB, BLOCK, KVH, GROUP, DH).transpose(2, 0, 1, 3, 4)
        results = lax.map(run_head, (query_heads, candidates))
        outputs.append(results.transpose(1, 2, 0, 3, 4).reshape(L, KVH * GROUP * DH))
    return jnp.stack(outputs)
```

```python
import functools
import math

import jax
import jax.numpy as jnp
from jax import lax
from jax.experimental import pallas as pl
from jax.experimental.pallas import tpu as pltpu
from jax.sharding import PartitionSpec as P

DH = 128
KVH = 8
GROUP = 4
BLOCK = 128


def attend_kernel(table_ref, q_ref, own_ref, first_ref, edge_ref, sorted_ref, out_ref):
    block = pl.program_id(0)
    before = jnp.where(block == 0, edge_ref[0], first_ref[0, 0])
    candidates = jnp.concatenate([own_ref[0, 0], before, sorted_ref[0]], axis=0)
    queries = jnp.concatenate([q_ref[:, g * DH : (g + 1) * DH] for g in range(GROUP)], axis=0)
    scores = lax.dot_general(
        queries, candidates[:, :DH], (((1,), (1,)), ((), ())), preferred_element_type=jnp.float32
    ) * (math.log2(math.e) / math.sqrt(DH))
    index = lax.broadcasted_iota(jnp.int32, scores.shape, 1)
    start = (table_ref[2 * KVH] == 0) & (block == 0)
    blocked = start & (index >= BLOCK) & (index < 2 * BLOCK)
    scores = jnp.where(blocked, -1e30, scores)
    raised = jnp.exp2(scores - jnp.max(scores, axis=-1, keepdims=True))
    weights = (raised * (1.0 / jnp.sum(raised, axis=-1, keepdims=True))).astype(jnp.bfloat16)
    result = jnp.dot(weights, candidates[:, DH:], preferred_element_type=jnp.float32).astype(jnp.bfloat16)
    for g in range(GROUP):
        out_ref[:, g * DH : (g + 1) * DH] = result[g * BLOCK : (g + 1) * BLOCK]


def attend(table, queries, packed, edge, arrived):
    rows, width = queries.shape
    span = GROUP * DH
    kv = (1, 1, BLOCK, 2 * DH)
    return pl.pallas_call(
        attend_kernel,
        out_shape=jax.ShapeDtypeStruct((rows, width), jnp.bfloat16),
        grid_spec=pltpu.PrefetchScalarGridSpec(
            num_scalar_prefetch=1,
            grid=(rows // BLOCK, KVH),
            in_specs=[
                pl.BlockSpec((BLOCK, span), lambda b, h, t: (b, h)),
                pl.BlockSpec(kv, lambda b, h, t: (b, h, 0, 0)),
                pl.BlockSpec(kv, lambda b, h, t: (0, h, 0, 0)),
                pl.BlockSpec(kv[1:], lambda b, h, t: (h, 0, 0)),
                pl.BlockSpec(kv[1:], lambda b, h, t: (t[h * 2 + b], 0, 0)),
            ],
            out_specs=pl.BlockSpec((BLOCK, span), lambda b, h, t: (b, h)),
        ),
        name="attend",
    )(table, queries, packed, packed, edge, arrived)


def local(tokens, queries, key_weight, value_weight, sorted_blocks):
    token_rows = tokens[0]
    local_blocks = token_rows.shape[0] // BLOCK
    devices = lax.axis_size("seq")
    axes = ("fsdp", "seq")
    targets = sorted_blocks[0]
    target_dev = (targets // local_blocks).reshape(-1)
    item = (targets % local_blocks) * KVH + jnp.arange(KVH, dtype=jnp.int32)[:, None]
    hit = target_dev[:, None] == jnp.arange(devices, dtype=jnp.int32)[None, :]
    requests = jnp.sum(jnp.where(hit, (item.reshape(-1) + 1)[:, None], 0), axis=0)
    wanted = lax.all_to_all(requests[:, None], "seq", split_axis=0, concat_axis=0, tiled=True)[:, 0]
    keys = jnp.dot(
        token_rows, lax.all_gather(key_weight, axes, axis=0, tiled=True), preferred_element_type=jnp.float32
    )
    values = jnp.dot(
        token_rows, lax.all_gather(value_weight, axes, axis=0, tiled=True), preferred_element_type=jnp.float32
    )
    keys = keys.astype(jnp.bfloat16).reshape(local_blocks, BLOCK, KVH, DH)
    values = values.astype(jnp.bfloat16).reshape(local_blocks, BLOCK, KVH, DH)
    packed = jnp.concatenate([keys, values], axis=3).transpose(0, 2, 1, 3)
    edge = lax.ppermute(packed[local_blocks - 1], "seq", [(s, s + 1) for s in range(devices - 1)])
    replies = jnp.take(
        packed.reshape(local_blocks * KVH, BLOCK, 2 * DH), jnp.maximum(wanted - 1, 0), axis=0, mode="clip"
    )
    arrived = lax.all_to_all(replies, "seq", split_axis=0, concat_axis=0, tiled=True)
    table = jnp.concatenate([target_dev, lax.axis_index("seq")[None]]).astype(jnp.int32)
    return attend(table, queries[0], packed, edge, arrived)[None]


def solution(mesh):
    placed = (
        P("fsdp", "seq", None),
        P("fsdp", "seq", None),
        P(("fsdp", "seq"), None),
        P(("fsdp", "seq"), None),
        P("fsdp", None, "seq"),
    )
    return jax.shard_map(
        local, mesh=mesh, in_specs=placed, out_specs=P("fsdp", "seq", None), check_vma=False
    )
```

```python
import functools
import math

import jax
import jax.numpy as jnp
from jax import lax
from jax.experimental import pallas as pl
from jax.experimental.pallas import tpu as pltpu
from jax.sharding import PartitionSpec as P

DH = 128
KVH = 8
GROUP = 4
BLOCK = 128


MESH = pl.DeviceIdType.MESH
AXES = ("x", "z", "y")


class Place:
    def __init__(self, sizes):
        self.sizes = sizes
        seq = lax.axis_index("seq")
        self.core = lax.rem(seq, 2)
        pair = lax.div(seq, 2)
        self.at = {"x": lax.axis_index("fsdp"), "y": lax.rem(pair, sizes["y"]), "z": lax.div(pair, sizes["y"])}

    def moved(self, axis, steps):
        return lax.rem(self.at[axis] + (steps % self.sizes[axis]), self.sizes[axis])

    def device(self, axis, steps):
        at = dict(self.at)
        at[axis] = self.moved(axis, steps)
        return (at["x"], (at["z"] * self.sizes["y"] + at["y"]) * 2 + self.core)

    def sibling(self):
        return (self.at["x"], (self.at["z"] * self.sizes["y"] + self.at["y"]) * 2 + 1 - self.core)


class Copies:
    def __init__(self, send_sem, recv_sem):
        self.send_sem, self.recv_sem = send_sem, recv_sem
        self.started = []

    def start(self, ref, device):
        slot = len(self.started)
        copy = pltpu.make_async_remote_copy(
            src_ref=ref, dst_ref=ref, send_sem=self.send_sem.at[slot], recv_sem=self.recv_sem.at[slot],
            device_id=device, device_id_type=MESH,
        )
        copy.start()
        self.started.append(copy)
        return slot, device

    def arrived(self, ticket, ref):
        slot, device = ticket
        pltpu.make_async_remote_copy(
            src_ref=ref, dst_ref=ref, send_sem=self.send_sem.at[slot], recv_sem=self.recv_sem.at[slot],
            device_id=device, device_id_type=MESH,
        ).wait_recv()

    def sent(self):
        for copy in self.started:
            copy.wait_send()


def run_tasks(tasks):
    queue = [[0.0, index, task] for index, task in enumerate(tasks)]
    while queue:
        queue.sort(key=lambda entry: entry[:2])
        entry = queue[0]
        try:
            wake, more = next(entry[2])
            entry[0] = wake
            for task in more:
                queue.append([wake, len(queue) + 1000, task])
        except StopIteration:
            queue.pop(0)


def gather_tasks(place, copies, gathered, part, order, width, handed):
    full = slice(None)

    def piece(where, half=None, core=None):
        cols = full if half is None else pl.ds(half * (width // 2), width // 2)
        at = [where[axis] for axis in AXES]
        return gathered.at[part, at[0], at[1], at[2], place.core if core is None else core, :, cols]

    def hand_over(where):
        ticket = copies.start(piece(where), place.sibling())
        handed.append((ticket, piece(where, core=1 - place.core)))

    def ring(axis, where, begin, span, on_arrival):
        half_way = place.sizes[axis] // 2
        ahead = copies.start(piece({**where, axis: place.at[axis]}), place.device(axis, 1))
        behind = copies.start(piece({**where, axis: place.at[axis]}), place.device(axis, -1))
        for step in range(1, half_way + 1):
            last = step == half_way
            before = {**where, axis: place.moved(axis, -step)}
            after = {**where, axis: place.moved(axis, step)}
            yield begin + step * span, []
            copies.arrived(ahead, piece(before, 0 if last else None))
            if not last:
                split = step + 1 == half_way
                ahead = copies.start(piece(before, 0 if split else None), place.device(axis, 1))
            copies.arrived(behind, piece(after, 1 if last else None))
            if not last:
                behind = copies.start(piece(after, 1 if split else None), place.device(axis, -1))
            for here in [after] if last else [before, after]:
                yield begin + step * span, on_arrival(here, begin + step * span)

    first, second, third = order

    def third_ring(where, begin):
        def on_arrival(here, time):
            hand_over(here)
            return []

        return ring(third, where, begin, 10.0, on_arrival)

    def spread(where, time):
        hand_over(where)
        return [third_ring({**where, third: full_at(third)}, time)]

    def full_at(axis):
        return place.at[axis]

    def whole():
        yield from ring(first, dict(place.at), 0.0, 2.0, lambda here, time: [])
        slab = {**place.at, first: full}
        yield 8.0, [ring(second, slab, 8.0, 8.0, spread)]
        hand_over(slab)
        yield 8.1, [third_ring(slab, 8.1)]

    return whole()


def project_kernel(sizes, tokens_ref, key_ref, value_ref, out_ref, gathered, rows, load_sem, send_sem, recv_sem):
    place = Place(sizes)
    width = key_ref.shape[1]
    at = [place.at[axis] for axis in AXES]
    loads = [
        pltpu.make_async_copy(ref, gathered.at[part, at[0], at[1], at[2], place.core], load_sem.at[part])
        for part, ref in enumerate((key_ref, value_ref))
    ]
    loads.append(pltpu.make_async_copy(tokens_ref, rows, load_sem.at[2]))
    for load in loads:
        load.start()
    barrier = pltpu.get_barrier_semaphore()
    neighbours = [place.device(axis, step) for axis in AXES for step in (1, -1)] + [place.sibling()]
    for device in neighbours:
        pl.semaphore_signal(barrier, inc=1, device_id=device, device_id_type=MESH)
    pl.semaphore_wait(barrier, len(neighbours))
    loads[0].wait()
    loads[1].wait()
    copies = Copies(send_sem, recv_sem)
    handed = []
    run_tasks([
        gather_tasks(place, copies, gathered, 0, ("z", "y", "x"), width, handed),
        gather_tasks(place, copies, gathered, 1, ("z", "x", "y"), width, handed),
    ])
    for ticket, ref in handed:
        copies.arrived(ticket, ref)
    loads[2].wait()
    depth = rows.shape[1]
    tile = 2 * DH

    def column_tile(step, carry):
        part = lax.div(step, width // tile)
        column = lax.rem(step, width // tile)
        cols = pl.ds(pl.multiple_of(column * tile, tile), tile)
        weight = gathered[part, :, :, :, :, :, cols].reshape(depth, tile)
        result = jnp.dot(rows[...], weight, preferred_element_type=jnp.float32).astype(jnp.bfloat16)
        lanes = pl.ds(pl.multiple_of(part * DH, DH), DH)
        for block in range(rows.shape[0] // BLOCK):
            for head in range(2):
                out_ref[block, column * 2 + head, :, lanes] = result[
                    block * BLOCK : (block + 1) * BLOCK, head * DH : (head + 1) * DH
                ]
        return carry

    lax.fori_loop(0, 2 * (width // tile), column_tile, 0)
    copies.sent()


def project(token_rows, key_weight, value_weight, sizes):
    local_tokens, depth = token_rows.shape
    part_rows, width = key_weight.shape
    blocks = local_tokens // BLOCK
    hbm = pl.BlockSpec(memory_space=pltpu.HBM)
    return pl.pallas_call(
        functools.partial(project_kernel, sizes),
        out_shape=jax.ShapeDtypeStruct((blocks, KVH, BLOCK, 2 * DH), jnp.bfloat16),
        in_specs=[hbm] * 3,
        out_specs=pl.BlockSpec(memory_space=pltpu.VMEM),
        scratch_shapes=[
            pltpu.VMEM((2, sizes["x"], sizes["z"], sizes["y"], 2, part_rows, width), jnp.bfloat16),
            pltpu.VMEM((local_tokens, depth), jnp.bfloat16),
            pltpu.SemaphoreType.DMA((3,)),
            pltpu.SemaphoreType.DMA((88,)),
            pltpu.SemaphoreType.DMA((88,)),
        ],
        compiler_params=pltpu.CompilerParams(
            collective_id=0, has_side_effects=True, vmem_limit_bytes=48 << 20
        ),
        name="project",
    )(token_rows, key_weight, value_weight)


def attend_kernel(table_ref, q_ref, own_ref, first_ref, edge_ref, sorted_ref, out_ref):
    block = pl.program_id(0)
    before = jnp.where(block == 0, edge_ref[0], first_ref[0, 0])
    candidates = jnp.concatenate([own_ref[0, 0], before, sorted_ref[0]], axis=0)
    queries = jnp.concatenate([q_ref[:, g * DH : (g + 1) * DH] for g in range(GROUP)], axis=0)
    scores = lax.dot_general(
        queries, candidates[:, :DH], (((1,), (1,)), ((), ())), preferred_element_type=jnp.float32
    ) * (math.log2(math.e) / math.sqrt(DH))
    index = lax.broadcasted_iota(jnp.int32, scores.shape, 1)
    start = (table_ref[2 * KVH] == 0) & (block == 0)
    blocked = start & (index >= BLOCK) & (index < 2 * BLOCK)
    scores = jnp.where(blocked, -1e30, scores)
    raised = jnp.exp2(scores - jnp.max(scores, axis=-1, keepdims=True))
    weights = (raised * (1.0 / jnp.sum(raised, axis=-1, keepdims=True))).astype(jnp.bfloat16)
    result = jnp.dot(weights, candidates[:, DH:], preferred_element_type=jnp.float32).astype(jnp.bfloat16)
    for g in range(GROUP):
        out_ref[:, g * DH : (g + 1) * DH] = result[g * BLOCK : (g + 1) * BLOCK]


def attend(table, queries, packed, edge, arrived):
    rows, width = queries.shape
    span = GROUP * DH
    kv = (1, 1, BLOCK, 2 * DH)
    return pl.pallas_call(
        attend_kernel,
        out_shape=jax.ShapeDtypeStruct((rows, width), jnp.bfloat16),
        grid_spec=pltpu.PrefetchScalarGridSpec(
            num_scalar_prefetch=1,
            grid=(rows // BLOCK, KVH),
            in_specs=[
                pl.BlockSpec((BLOCK, span), lambda b, h, t: (b, h)),
                pl.BlockSpec(kv, lambda b, h, t: (b, h, 0, 0)),
                pl.BlockSpec(kv, lambda b, h, t: (0, h, 0, 0)),
                pl.BlockSpec(kv[1:], lambda b, h, t: (h, 0, 0)),
                pl.BlockSpec(kv[1:], lambda b, h, t: (t[h * 2 + b], 0, 0)),
            ],
            out_specs=pl.BlockSpec((BLOCK, span), lambda b, h, t: (b, h)),
        ),
        name="attend",
    )(table, queries, packed, packed, edge, arrived)


def local(tokens, queries, key_weight, value_weight, sorted_blocks):
    token_rows = tokens[0]
    local_blocks = token_rows.shape[0] // BLOCK
    devices = lax.axis_size("seq")
    targets = sorted_blocks[0]
    target_dev = (targets // local_blocks).reshape(-1)
    item = (targets % local_blocks) * KVH + jnp.arange(KVH, dtype=jnp.int32)[:, None]
    hit = target_dev[:, None] == jnp.arange(devices, dtype=jnp.int32)[None, :]
    requests = jnp.sum(jnp.where(hit, (item.reshape(-1) + 1)[:, None], 0), axis=0)
    wanted = lax.all_to_all(requests[:, None], "seq", split_axis=0, concat_axis=0, tiled=True)[:, 0]
    sizes = {"x": lax.axis_size("fsdp"), "y": 4, "z": devices // 8}
    packed = project(token_rows, key_weight, value_weight, sizes)
    edge = lax.ppermute(packed[local_blocks - 1], "seq", [(s, s + 1) for s in range(devices - 1)])
    replies = jnp.take(
        packed.reshape(local_blocks * KVH, BLOCK, 2 * DH), jnp.maximum(wanted - 1, 0), axis=0, mode="clip"
    )
    arrived = lax.all_to_all(replies, "seq", split_axis=0, concat_axis=0, tiled=True)
    table = jnp.concatenate([target_dev, lax.axis_index("seq")[None]]).astype(jnp.int32)
    return attend(table, queries[0], packed, edge, arrived)[None]


def solution(mesh):
    placed = (
        P("fsdp", "seq", None),
        P("fsdp", "seq", None),
        P(("fsdp", "seq"), None),
        P(("fsdp", "seq"), None),
        P("fsdp", None, "seq"),
    )
    return jax.shard_map(
        local, mesh=mesh, in_specs=placed, out_specs=P("fsdp", "seq", None), check_vma=False
    )
```

```python
import functools
import math

import jax
import jax.numpy as jnp
from jax import lax
from jax.experimental import pallas as pl
from jax.experimental.pallas import tpu as pltpu
from jax.sharding import PartitionSpec as P

DH = 128
KVH = 8
GROUP = 4
BLOCK = 128
MESH = pl.DeviceIdType.MESH
AXES = ("x", "z", "y")
FULL = slice(None)
LANES = 128
STAGES = ((0, 3), (3, 5), (5, 7), (7, 8))


class Place:
    def __init__(self, sizes):
        self.sizes = sizes
        self.seq = lax.axis_index("seq")
        self.core = lax.rem(self.seq, 2)
        pair = lax.div(self.seq, 2)
        self.at = {"x": lax.axis_index("fsdp"), "y": lax.rem(pair, sizes["y"]), "z": lax.div(pair, sizes["y"])}
        self.columns = 2 * sizes["y"]
        self.column = self.at["y"] * 2 + self.core

    def moved(self, axis, steps):
        return lax.rem(self.at[axis] + (steps % self.sizes[axis]), self.sizes[axis])

    def device(self, axis, steps):
        at = dict(self.at)
        at[axis] = self.moved(axis, steps)
        return (at["x"], (at["z"] * self.sizes["y"] + at["y"]) * 2 + self.core)

    def sibling(self):
        return (self.at["x"], self.at["z"] * self.columns + self.at["y"] * 2 + 1 - self.core)

    def other_column(self, steps):
        return lax.rem(self.column + (steps % self.columns), self.columns)

    def in_row(self, steps):
        return (self.at["x"], self.at["z"] * self.columns + self.other_column(steps))

    def along(self, steps):
        count = self.sizes["z"] * self.columns
        return (self.at["x"], lax.rem(self.seq + (steps % count), count))


class Copies:
    def __init__(self, send_sem, recv_sem):
        self.send_sem, self.recv_sem = send_sem, recv_sem
        self.started = []

    def make(self, slot, source, target, device):
        return pltpu.make_async_remote_copy(
            src_ref=source, dst_ref=target, send_sem=self.send_sem.at[slot], recv_sem=self.recv_sem.at[slot],
            device_id=device, device_id_type=MESH,
        )

    def start(self, source, target, device):
        slot = len(self.started)
        copy = self.make(slot, source, target, device)
        copy.start()
        self.started.append(copy)
        return slot, device

    def arrived(self, ticket, target):
        self.make(ticket[0], target, target, ticket[1]).wait_recv()

    def sent(self):
        for copy in self.started:
            copy.wait_send()


def run_tasks(tasks):
    count = 0
    queue = []
    for task in tasks:
        queue.append([0.0, count, task])
        count += 1
    while queue:
        queue.sort(key=lambda entry: entry[:2])
        entry = queue[0]
        try:
            wake, more = next(entry[2])
            entry[0] = wake
            for task in more:
                queue.append([wake, count, task])
                count += 1
        except StopIteration:
            queue.pop(0)


class Group:
    def __init__(self, then):
        self.open, self.then = 0, then

    def add(self, task):
        self.open += 1

        def run():
            wake = 0.0
            for wake, more in task:
                yield wake, more
            self.open -= 1
            if self.open == 0:
                yield wake, self.then(wake)

        return run()


def ring(place, copies, piece, axis, where, begin, span, on_arrival, halves=True):
    half_way = place.sizes[axis] // 2
    yield begin, []
    own = piece({**where, axis: place.at[axis]}, None)
    ahead = copies.start(own, own, place.device(axis, 1))
    behind = copies.start(own, own, place.device(axis, -1))
    for step in range(1, half_way + 1):
        last, split = step == half_way, step + 1 == half_way
        before = {**where, axis: place.moved(axis, -step)}
        after = {**where, axis: place.moved(axis, step)}
        time = begin + step * span
        yield time, []
        copies.arrived(ahead, piece(before, 0 if last and halves else None))
        if not last:
            ref = piece(before, 0 if split and halves else None)
            ahead = copies.start(ref, ref, place.device(axis, 1))
        if not last or halves:
            copies.arrived(behind, piece(after, 1 if last else None))
        if not last and not (split and not halves):
            ref = piece(after, 1 if split else None)
            behind = copies.start(ref, ref, place.device(axis, -1))
        for here in [after] if last else [before, after]:
            more = on_arrival(here, time)
            if more:
                yield time, more


def gather_weight(place, copies, group, weights, kind, part, order, ready, begin, spans):
    first, second, third = order

    def piece(where, half):
        rows = FULL if half is None else pl.ds(half * 16, 16)
        at = [where[axis] for axis in AXES]
        return weights.at[kind, part, at[0], at[1], at[2], rows, :]

    def nothing(here, time):
        return []

    def third_ring(where, time):
        return group.add(ring(place, copies, piece, third, {**where, third: place.at[third]}, time, spans[2], nothing))

    def whole():
        yield begin[0], []
        ready(kind, part)
        yield from ring(place, copies, piece, first, dict(place.at), begin[0], spans[0], nothing)
        slab = {**place.at, first: FULL}
        yield begin[1], [
            group.add(ring(place, copies, piece, second, slab, begin[1], spans[1], lambda here, time: [third_ring(here, time)])),
            third_ring(slab, begin[1]),
        ]

    return group.add(whole())


class Kind:
    names = ("own", "back1", "ahead1", "back2", "ahead2", "swap", "edge", "far_out", "far_back", "far_ahead", "last", "slots", "arrived")

    def __init__(self, refs):
        for name, ref in zip(self.names, refs):
            setattr(self, name, ref)

    @classmethod
    def scratch(cls, rows, columns):
        half = KVH // 2
        block = (BLOCK, DH)
        shapes = [(2, KVH)] * 5 + [(2, half), (KVH,), (2, columns + columns // 2)]
        shapes += [(columns + columns // 2,)] * 2 + [(2, columns // 2), (columns - 1, rows), (columns, rows)]
        return [pltpu.VMEM(shape + block, jnp.bfloat16) for shape in shapes]


def layer_kernel(sizes, plan, sorted_ref, list_ref, tokens_ref, queries_ref, key_ref, value_ref, out_ref,
                 weights, tokens, queries, lists, wanted_vector, wanted, softmax, *rest):
    kinds = [Kind(rest[:13]), Kind(rest[13:26])]
    load_sem, send_sem, recv_sem = rest[26:]
    place = Place(sizes)
    copies = Copies(send_sem, recv_sem)
    x, z, y, core = place.at["x"], place.at["z"], place.at["y"], place.core
    columns, rows_z = place.columns, sizes["z"]
    half_width = key_ref.shape[1] // 2
    part_width = half_width // 2

    loads = {}

    def load(name, source, target):
        loads[name] = pltpu.make_async_copy(source, target, load_sem.at[len(loads)])
        loads[name].start()

    def weight_columns(ref, which, part):
        return ref.at[:, pl.ds(pl.multiple_of(which * half_width + part * part_width, part_width), part_width)]

    for kind, ref in enumerate((key_ref, value_ref)):
        for part in range(2):
            load((kind, part), weight_columns(ref, core, part), weights.at[kind, part, x, z, y, pl.ds(core * 16, 16), :])
    load("lists", list_ref, lists.at[z, y, core])
    load("tokens", tokens_ref, tokens.at[core])
    load("queries", queries_ref, queries)

    barrier = pltpu.get_barrier_semaphore()
    peers = [place.device(axis, step) for axis in ("x", "z") for step in (1, -1)]
    peers += [place.in_row(step) for step in range(1, columns)]
    peers += [place.along(1), place.along(-1)]
    for device in peers:
        pl.semaphore_signal(barrier, inc=1, device_id=device, device_id_type=MESH)
    pl.semaphore_wait(barrier, len(peers))

    shared = {}
    for kind, ref in enumerate((key_ref, value_ref)):
        for part in range(2):
            shared[kind, part] = copies.start(
                weight_columns(ref, 1 - core, part), weights.at[kind, part, x, z, y, pl.ds(core * 16, 16), :], place.sibling()
            )
    shared["tokens"] = copies.start(tokens_ref, tokens.at[core], place.sibling())

    def ready(kind, part):
        loads[kind, part].wait()
        copies.arrived(shared[kind, part], weights.at[kind, part, x, z, y, pl.ds((1 - core) * 16, 16), :])

    def list_task():
        def piece(where, half):
            return lists.at[where["z"], where["y"], core]

        def nothing(here, time):
            return []

        loads["lists"].wait()
        yield from ring(place, copies, piece, "z", dict(place.at), 0.0, 2.0, nothing, halves=False)
        yield from ring(place, copies, piece, "y", {**place.at, "z": FULL}, 8.0, 2.0, nothing, halves=False)
        mine = lists.at[:, :, core]
        ticket = copies.start(mine, mine, place.sibling())
        yield 14.5, []
        copies.arrived(ticket, lists.at[:, :, 1 - core])
        lane = lax.broadcasted_iota(jnp.int32, (8, LANES), 1)
        source = lax.broadcasted_iota(jnp.int32, (8, LANES), 0) * columns + place.column

        def one_device(device, total):
            tile = lists[lax.div(device, columns), lax.div(lax.rem(device, columns), 2), lax.rem(device, 2)]
            item = (tile & 1) * KVH + (lane >> 1) + 1
            found = jnp.sum(jnp.where((tile >> 1) == source, item, 0), axis=1, keepdims=True)
            return jnp.where(lane == device, found, total)

        wanted_vector[...] = lax.fori_loop(0, rows_z * columns, one_device, jnp.zeros((8, LANES), jnp.int32))
        copy = pltpu.make_async_copy(wanted_vector, wanted, load_sem.at[len(loads)])
        copy.start()
        copy.wait()

    def picked(ref, steps, row_steps, column):
        device = place.moved("z", row_steps) * columns + column
        item = jnp.clip(wanted[place.moved("z", steps), device] - 1, 0, 2 * KVH - 1)
        return ref[lax.div(item, KVH), lax.rem(item, KVH)]

    def project(kind):
        buffers = kinds[kind]
        if kind == 0:
            loads["tokens"].wait()
            copies.arrived(shared["tokens"], tokens.at[1 - core])
        for part in range(2):
            weight = weights[kind, part].reshape(tokens.shape[2], part_width)
            for mine in (False, True):
                which = core if mine else 1 - core
                result = jnp.dot(tokens[which], weight, preferred_element_type=jnp.float32).astype(jnp.bfloat16)
                for block in range(2):
                    for head in range(2):
                        value = result[block * BLOCK : (block + 1) * BLOCK, head * DH : (head + 1) * DH]
                        if mine:
                            buffers.own[block, core * (KVH // 2) + part * 2 + head] = value
                        else:
                            buffers.swap[block, part * 2 + head] = value
        return copies.start(buffers.swap, buffers.own.at[:, pl.ds(core * (KVH // 2), KVH // 2)], place.sibling())

    def send_slots(buffers, stage, row_tickets):
        begin, end = STAGES[stage]
        sources = {0: (buffers.own, 0), 1: (buffers.back1, -1), 2: (buffers.ahead1, 1), 3: (buffers.back2, -2), 4: (buffers.ahead2, 2)}

        def value(slot, column):
            if slot < 5:
                return picked(*sources[slot], 0, column)
            if slot == 5:
                return buffers.far_back[column]
            if slot == 6:
                return buffers.far_ahead[column]
            return buffers.last[lax.rem(column, 2), lax.div(column, 2)]

        for slot in range(begin, end):
            buffers.arrived[place.column, slot] = value(slot, place.column)
        for step in range(1, columns):
            column = place.other_column(step)
            for slot in range(begin, end):
                buffers.slots[step - 1, slot] = value(slot, column)
            ticket = copies.start(
                buffers.slots.at[step - 1, pl.ds(begin, end - begin)],
                buffers.arrived.at[place.column, pl.ds(begin, end - begin)],
                place.in_row(step),
            )
            row_tickets.append((ticket, buffers.arrived.at[place.other_column(-step), pl.ds(begin, end - begin)]))

    def send_far(buffers, direction):
        ref = buffers.back2 if direction == 1 else buffers.ahead2
        side = 0 if direction == 1 else 1
        for column in range(columns):
            buffers.far_out[side, column] = picked(ref, -2 * direction, direction, column)
        for index in range(columns // 2):
            buffers.far_out[side, columns + index] = picked(ref, -2 * direction, 2 * direction, 2 * index + side)
        target = buffers.far_back if direction == 1 else buffers.far_ahead
        return copies.start(buffers.far_out.at[side], target, place.device("z", direction))

    def exchange(kind, then):
        times = plan["exchange"][kind]

        def task():
            buffers = kinds[kind]
            row_tickets = []
            ticket = project(kind)
            yield times[0], []
            copies.arrived(ticket, buffers.own.at[:, pl.ds((1 - core) * (KVH // 2), KVH // 2)])
            ahead = copies.start(buffers.own, buffers.back1, place.device("z", 1))
            behind = copies.start(buffers.own, buffers.ahead1, place.device("z", -1))
            edge = copies.start(buffers.own.at[1], buffers.edge, place.along(1))
            yield times[1], []
            copies.arrived(ahead, buffers.back1)
            ahead = copies.start(buffers.back1, buffers.back2, place.device("z", 1))
            copies.arrived(behind, buffers.ahead1)
            behind = copies.start(buffers.ahead1, buffers.ahead2, place.device("z", -1))
            send_slots(buffers, 0, row_tickets)
            yield times[2], []
            copies.arrived(ahead, buffers.back2)
            ahead = send_far(buffers, 1)
            copies.arrived(behind, buffers.ahead2)
            behind = send_far(buffers, -1)
            send_slots(buffers, 1, row_tickets)
            yield times[3], []
            tail = pl.ds(columns, columns // 2)
            copies.arrived(ahead, buffers.far_back)
            ahead = copies.start(buffers.far_back.at[tail], buffers.last.at[0], place.device("z", 1))
            copies.arrived(behind, buffers.far_ahead)
            behind = copies.start(buffers.far_ahead.at[tail], buffers.last.at[1], place.device("z", -1))
            send_slots(buffers, 2, row_tickets)
            yield times[4], []
            copies.arrived(ahead, buffers.last.at[0])
            copies.arrived(behind, buffers.last.at[1])
            send_slots(buffers, 3, row_tickets)
            yield times[5], []
            copies.arrived(edge, buffers.edge)
            for ticket, target in row_tickets:
                copies.arrived(ticket, target)
            yield times[5], then

        return [task()]

    def candidates(kind, block, head):
        buffers = kinds[kind]
        device = lax.div(sorted_ref[head, block], 2)
        distance = lax.rem(lax.div(device, columns) - z + rows_z, rows_z)
        slot = jnp.where(
            distance < 4, 2 * distance, jnp.where(distance == 4, 7, 2 * (rows_z - distance) - 1)
        )
        before = buffers.edge[head] if block == 0 else buffers.own[0, head]
        return jnp.concatenate(
            [buffers.own[block, head], before, buffers.arrived[lax.rem(device, columns), slot]], axis=0
        )

    def weights_task(block, head_range, wake):
        def one_head(head, carry):
            rows = slice(block * BLOCK, (block + 1) * BLOCK)
            query = queries[rows, pl.ds(pl.multiple_of(head * GROUP * DH, GROUP * DH), GROUP * DH)]
            query = jnp.concatenate([query[:, g * DH : (g + 1) * DH] for g in range(GROUP)], axis=0)
            scores = lax.dot_general(
                query, candidates(0, block, head), (((1,), (1,)), ((), ())), preferred_element_type=jnp.float32
            ) * (math.log2(math.e) / math.sqrt(DH))
            if block == 0:
                index = lax.broadcasted_iota(jnp.int32, scores.shape, 1)
                blocked = (place.seq == 0) & (index >= BLOCK) & (index < 2 * BLOCK)
                scores = jnp.where(blocked, -1e30, scores)
            raised = jnp.exp2(scores - jnp.max(scores, axis=-1, keepdims=True))
            scale = 1.0 / jnp.sum(raised, axis=-1, keepdims=True)
            softmax[block * KVH + head] = (raised * scale).astype(jnp.bfloat16)
            return carry

        yield wake, []
        if block == 0 and head_range[0] == 0:
            loads["queries"].wait()
        lax.fori_loop(*head_range, one_head, 0)

    def output_task():
        yield plan["output"], []
        for block in range(2):

            def one_head(head, carry, block=block):
                result = jnp.dot(
                    softmax[block * KVH + head], candidates(1, block, head), preferred_element_type=jnp.float32
                ).astype(jnp.bfloat16)
                for g in range(GROUP):
                    lanes = pl.ds(pl.multiple_of((head * GROUP + g) * DH, DH), DH)
                    out_ref[block * BLOCK : (block + 1) * BLOCK, lanes] = result[g * BLOCK : (g + 1) * BLOCK]
                return carry

            lax.fori_loop(0, KVH, one_head, 0)

    half = KVH // 2
    both = Group(lambda wake: [output_task()])
    softmax_tasks = [
        both.add(weights_task(block, (begin, begin + half), plan["softmax"][block * 2 + begin // half]))
        for block in range(2) for begin in (0, half)
    ]
    values_ready = both.add(iter(()))
    groups = [
        Group(lambda wake: exchange(0, softmax_tasks)),
        Group(lambda wake: exchange(1, [values_ready])),
    ]
    tasks = [list_task()]
    for kind in range(2):
        for part, order in enumerate((("z", "y", "x"), ("z", "x", "y"))):
            tasks.append(
                gather_weight(place, copies, groups[kind], weights, kind, part, order, ready, plan["begin"][kind], plan["spans"])
            )
    run_tasks(tasks)
    copies.sent()
    assert len(copies.started) == COPIES, len(copies.started)


PLAN = {
    "begin": ((0.0, 10.0), (0.5, 27.0)),
    "spans": (2.0, 5.0, 8.0),
    "exchange": ((36.0, 48.0, 60.0, 69.0, 73.0, 78.0), (64.0, 82.0, 94.0, 104.0, 108.0, 114.0)),
    "softmax": (78.5, 82.5, 86.0, 95.0),
    "output": 115.0,
}


def layer(sorted_blocks, lists, tokens, queries, key_weight, value_weight, sizes):
    local_tokens, depth = tokens.shape
    part_rows, width = key_weight.shape
    columns, rows = 2 * sizes["y"], sizes["z"]
    hbm = pl.BlockSpec(memory_space=pltpu.HBM)
    kind = Kind.scratch(rows, columns)
    return pl.pallas_call(
        functools.partial(layer_kernel, sizes, PLAN),
        out_shape=jax.ShapeDtypeStruct(queries.shape, jnp.bfloat16),
        in_specs=[pl.BlockSpec(memory_space=pltpu.SMEM)] + [hbm] * 5,
        out_specs=pl.BlockSpec(memory_space=pltpu.VMEM),
        scratch_shapes=[
            pltpu.VMEM((2, 2, sizes["x"], rows, sizes["y"], 2 * part_rows, width // 4), jnp.bfloat16),
            pltpu.VMEM((2, local_tokens, depth), jnp.bfloat16),
            pltpu.VMEM(queries.shape, jnp.bfloat16),
            pltpu.VMEM((rows, sizes["y"], 2, 8, LANES), jnp.int32),
            pltpu.VMEM((8, LANES), jnp.int32),
            pltpu.SMEM((8, LANES), jnp.int32),
            pltpu.VMEM((2 * KVH, GROUP * BLOCK, 3 * BLOCK), jnp.bfloat16),
            *kind,
            *kind,
            pltpu.SemaphoreType.DMA((8,)),
            pltpu.SemaphoreType.DMA((COPIES,)),
            pltpu.SemaphoreType.DMA((COPIES,)),
        ],
        compiler_params=pltpu.CompilerParams(
            collective_id=0, has_side_effects=True, vmem_limit_bytes=58 << 20
        ),
        name="layer",
    )(sorted_blocks, lists, tokens, queries, key_weight, value_weight)


COPIES = 204


def local(tokens, queries, key_weight, value_weight, sorted_blocks):
    devices = lax.axis_size("seq")
    sizes = {"x": lax.axis_size("fsdp"), "y": 4, "z": devices // 8}
    own = sorted_blocks[0].reshape(-1)
    lists = jnp.broadcast_to(jnp.pad(own, (0, LANES - own.shape[0]), constant_values=-1), (8, LANES))
    return layer(sorted_blocks[0], lists, tokens[0], queries[0], key_weight, value_weight, sizes)[None]


def solution(mesh):
    placed = (
        P("fsdp", "seq", None),
        P("fsdp", "seq", None),
        P(("fsdp", "seq"), None),
        P(("fsdp", "seq"), None),
        P("fsdp", None, "seq"),
    )
    return jax.shard_map(
        local, mesh=mesh, in_specs=placed, out_specs=P("fsdp", "seq", None), check_vma=False
    )
```

```python
import functools
import math

import jax
import jax.numpy as jnp
from jax import lax
from jax.experimental import pallas as pl
from jax.experimental.pallas import tpu as pltpu
from jax.sharding import PartitionSpec as P

DH = 128
KVH = 8
GROUP = 4
BLOCK = 128
MESH = pl.DeviceIdType.MESH
AXES = ("x", "z", "y")
FULL = slice(None)
LANES = 128
STAGES = ((0, 3), (3, 5), (5, 7), (7, 8))


class Place:
    def __init__(self, sizes):
        self.sizes = sizes
        self.seq = lax.axis_index("seq")
        self.core = lax.rem(self.seq, 2)
        pair = lax.div(self.seq, 2)
        self.at = {"x": lax.axis_index("fsdp"), "y": lax.rem(pair, sizes["y"]), "z": lax.div(pair, sizes["y"])}
        self.columns = 2 * sizes["y"]
        self.column = self.at["y"] * 2 + self.core

    def moved(self, axis, steps):
        return lax.rem(self.at[axis] + (steps % self.sizes[axis]), self.sizes[axis])

    def device(self, axis, steps):
        at = dict(self.at)
        at[axis] = self.moved(axis, steps)
        return (at["x"], (at["z"] * self.sizes["y"] + at["y"]) * 2 + self.core)

    def sibling(self):
        return (self.at["x"], self.at["z"] * self.columns + self.at["y"] * 2 + 1 - self.core)

    def other_column(self, steps):
        return lax.rem(self.column + (steps % self.columns), self.columns)

    def in_row(self, steps):
        return (self.at["x"], self.at["z"] * self.columns + self.other_column(steps))

    def along(self, steps):
        count = self.sizes["z"] * self.columns
        return (self.at["x"], lax.rem(self.seq + (steps % count), count))


class Copies:
    def __init__(self, send_sem, recv_sem):
        self.send_sem, self.recv_sem = send_sem, recv_sem
        self.started = []

    def make(self, slot, source, target, device):
        return pltpu.make_async_remote_copy(
            src_ref=source, dst_ref=target, send_sem=self.send_sem.at[slot], recv_sem=self.recv_sem.at[slot],
            device_id=device, device_id_type=MESH,
        )

    def start(self, source, target, device):
        slot = len(self.started)
        copy = self.make(slot, source, target, device)
        copy.start()
        self.started.append(copy)
        return slot, device

    def arrived(self, ticket, target):
        self.make(ticket[0], target, target, ticket[1]).wait_recv()

    def sent(self):
        for copy in self.started:
            copy.wait_send()


def run_tasks(tasks):
    count = 0
    queue = []
    for task in tasks:
        queue.append([0.0, count, task])
        count += 1
    while queue:
        queue.sort(key=lambda entry: entry[:2])
        entry = queue[0]
        try:
            wake, more = next(entry[2])
            entry[0] = wake
            for task in more:
                queue.append([wake, count, task])
                count += 1
        except StopIteration:
            queue.pop(0)


class Group:
    def __init__(self, then):
        self.open, self.then = 0, then

    def add(self, task):
        self.open += 1

        def run():
            wake = 0.0
            for wake, more in task:
                yield wake, more
            self.open -= 1
            if self.open == 0:
                yield wake, self.then(wake)

        return run()


def ring(place, copies, piece, axis, where, begin, span, on_arrival, halves=True):
    half_way = place.sizes[axis] // 2
    yield begin, []
    own = piece({**where, axis: place.at[axis]}, None)
    ahead = copies.start(own, own, place.device(axis, 1))
    behind = copies.start(own, own, place.device(axis, -1))
    for step in range(1, half_way + 1):
        last, split = step == half_way, step + 1 == half_way
        before = {**where, axis: place.moved(axis, -step)}
        after = {**where, axis: place.moved(axis, step)}
        time = begin + step * span
        yield time, []
        copies.arrived(ahead, piece(before, 0 if last and halves else None))
        if not last:
            ref = piece(before, 0 if split and halves else None)
            ahead = copies.start(ref, ref, place.device(axis, 1))
        if not last or halves:
            copies.arrived(behind, piece(after, 1 if last else None))
        if not last and not (split and not halves):
            ref = piece(after, 1 if split else None)
            behind = copies.start(ref, ref, place.device(axis, -1))
        for here in [after] if last else [before, after]:
            more = on_arrival(here, time)
            if more:
                yield time, more


def gather_weight(place, copies, group, weights, kind, part, axes, begin, spans):
    second, third = axes
    width = weights.shape[-1] // 2

    def piece(where, half):
        rows = FULL if half is None else pl.ds(half * 16, 16)
        return weights.at[kind, where["x"], :, where["y"], rows, pl.ds(part * width, width)]

    def nothing(here, time):
        return []

    def third_ring(where, time):
        return group.add(ring(place, copies, piece, third, {**where, third: place.at[third]}, time, spans[2], nothing))

    def whole():
        yield begin, [
            group.add(ring(place, copies, piece, second, dict(place.at), begin, spans[1], lambda here, time: [third_ring(here, time)])),
            third_ring(dict(place.at), begin),
        ]

    return group.add(whole())


class Kind:
    names = ("own", "back1", "ahead1", "back2", "ahead2", "swap", "edge", "far_out", "far_back", "far_ahead", "last", "slots", "arrived")

    def __init__(self, refs):
        for name, ref in zip(self.names, refs):
            setattr(self, name, ref)

    @classmethod
    def scratch(cls, rows, columns):
        half = KVH // 2
        block = (BLOCK, DH)
        shapes = [(2, KVH)] * 5 + [(2, half), (KVH,), (2, columns + columns // 2)]
        shapes += [(columns + columns // 2,)] * 2 + [(2, columns // 2), (columns - 1, rows), (columns, rows)]
        return [pltpu.VMEM(shape + block, jnp.bfloat16) for shape in shapes]


def layer_kernel(sizes, plan, list_ref, tokens_ref, queries_ref, key_ref, value_ref, out_ref,
                 weights, tokens, queries, lists, wanted_vector, wanted, own_list, softmax, *rest):
    kinds = [Kind(rest[:13]), Kind(rest[13:26])]
    load_sem, send_sem, recv_sem = rest[26:]
    place = Place(sizes)
    copies = Copies(send_sem, recv_sem)
    x, z, y, core = place.at["x"], place.at["z"], place.at["y"], place.core
    columns, rows_z = place.columns, sizes["z"]
    half_width = key_ref.shape[1] // 2
    part_width = half_width // 2

    loads = {}

    def load(name, source, target):
        loads[name] = pltpu.make_async_copy(source, target, load_sem.at[len(loads)])
        loads[name].start()

    def weight_columns(ref, which):
        return ref.at[:, pl.ds(pl.multiple_of(which * half_width, half_width), half_width)]

    def weight_rows(kind, which):
        return weights.at[kind, x, z, y, pl.ds(which * 16, 16), :]

    weight_refs = (key_ref, value_ref)
    for kind in range(2):
        load(kind, weight_columns(weight_refs[kind], core), weight_rows(kind, core))
    load("own_list", list_ref, own_list)
    load("lists", list_ref, lists.at[z, y, core])
    load("tokens", tokens_ref, tokens.at[core])
    load("queries", queries_ref, queries)

    barrier = pltpu.get_barrier_semaphore()
    peers = [place.device(axis, step) for axis in ("x", "z") for step in (1, -1)]
    peers += [place.in_row(step) for step in range(1, columns)]
    peers += [place.along(1), place.along(-1)]
    for device in peers:
        pl.semaphore_signal(barrier, inc=1, device_id=device, device_id_type=MESH)
    pl.semaphore_wait(barrier, len(peers))

    shared = {}
    for kind in range(2):
        shared[kind] = copies.start(
            weight_columns(weight_refs[kind], 1 - core), weight_rows(kind, core), place.sibling()
        )
    shared["tokens"] = copies.start(tokens_ref, tokens.at[core], place.sibling())

    def first_task(then):
        for kind in range(2):
            loads[kind].wait()
            copies.arrived(shared[kind], weight_rows(kind, 1 - core))

        def piece(where, half):
            rows = FULL if half is None else pl.ds(half * 16, 16)
            return weights.at[:, where["x"], where["z"], where["y"], rows, :]

        yield from ring(place, copies, piece, "z", dict(place.at), *plan["first"], lambda here, time: [])
        yield plan["first"][0] + 4 * plan["first"][1], then

    def list_task():
        def piece(where, half):
            return lists.at[where["z"], where["y"], core]

        def nothing(here, time):
            return []

        loads["lists"].wait()
        yield from ring(place, copies, piece, "z", dict(place.at), *plan["lists"][0], nothing, halves=False)
        yield from ring(place, copies, piece, "y", {**place.at, "z": FULL}, *plan["lists"][1], nothing, halves=False)
        mine = lists.at[:, :, core]
        ticket = copies.start(mine, mine, place.sibling())
        yield plan["lists"][2], []
        copies.arrived(ticket, lists.at[:, :, 1 - core])
        lane = lax.broadcasted_iota(jnp.int32, (8, LANES), 1)
        source = lax.broadcasted_iota(jnp.int32, (8, LANES), 0) * columns + place.column

        def one_device(device, total):
            tile = lists[lax.div(device, columns), lax.div(lax.rem(device, columns), 2), lax.rem(device, 2)]
            item = (tile & 1) * KVH + (lane & 7) + 1
            found = jnp.sum(jnp.where((tile >> 1) == source, item, 0), axis=1, keepdims=True)
            return jnp.where(lane == device, found, total)

        wanted_vector[...] = lax.fori_loop(0, rows_z * columns, one_device, jnp.zeros((8, LANES), jnp.int32), unroll=8)
        copy = pltpu.make_async_copy(wanted_vector, wanted, load_sem.at[len(loads)])
        copy.start()
        copy.wait()

    def picked(ref, steps, row_steps, column):
        device = place.moved("z", row_steps) * columns + column
        item = jnp.clip(wanted[place.moved("z", steps), device] - 1, 0, 2 * KVH - 1)
        return ref[lax.div(item, KVH), lax.rem(item, KVH)]

    def project(kind):
        buffers = kinds[kind]
        if kind == 0:
            loads["tokens"].wait()
            copies.arrived(shared["tokens"], tokens.at[1 - core])
        for part in range(2):
            weight = weights[kind, :, :, :, :, part * part_width : (part + 1) * part_width].reshape(tokens.shape[2], part_width)
            for mine in (False, True):
                which = core if mine else 1 - core
                result = jnp.dot(tokens[which], weight, preferred_element_type=jnp.float32).astype(jnp.bfloat16)
                for block in range(2):
                    for head in range(2):
                        value = result[block * BLOCK : (block + 1) * BLOCK, head * DH : (head + 1) * DH]
                        if mine:
                            buffers.own[block, core * (KVH // 2) + part * 2 + head] = value
                        else:
                            buffers.swap[block, part * 2 + head] = value
        return copies.start(buffers.swap, buffers.own.at[:, pl.ds(core * (KVH // 2), KVH // 2)], place.sibling())

    def send_slots(buffers, stage, row_tickets):
        begin, end = STAGES[stage]
        sources = {0: (buffers.own, 0), 1: (buffers.back1, -1), 2: (buffers.ahead1, 1), 3: (buffers.back2, -2), 4: (buffers.ahead2, 2)}

        def value(slot, column):
            if slot < 5:
                return picked(*sources[slot], 0, column)
            if slot == 5:
                return buffers.far_back[column]
            if slot == 6:
                return buffers.far_ahead[column]
            return buffers.last[lax.rem(column, 2), lax.div(column, 2)]

        for slot in range(begin, end):
            buffers.arrived[place.column, slot] = value(slot, place.column)
        for step in range(1, columns):
            column = place.other_column(step)
            for slot in range(begin, end):
                buffers.slots[step - 1, slot] = value(slot, column)
            ticket = copies.start(
                buffers.slots.at[step - 1, pl.ds(begin, end - begin)],
                buffers.arrived.at[place.column, pl.ds(begin, end - begin)],
                place.in_row(step),
            )
            row_tickets.append((ticket, buffers.arrived.at[place.other_column(-step), pl.ds(begin, end - begin)]))

    def send_far(buffers, direction):
        ref = buffers.back2 if direction == 1 else buffers.ahead2
        side = 0 if direction == 1 else 1
        for column in range(columns):
            buffers.far_out[side, column] = picked(ref, -2 * direction, direction, column)
        for index in range(columns // 2):
            buffers.far_out[side, columns + index] = picked(ref, -2 * direction, 2 * direction, 2 * index + side)
        target = buffers.far_back if direction == 1 else buffers.far_ahead
        return copies.start(buffers.far_out.at[side], target, place.device("z", direction))

    def exchange(kind, then):
        times = plan["exchange"][kind]

        def task():
            buffers = kinds[kind]
            row_tickets = []
            ticket = project(kind)
            yield times[0], []
            copies.arrived(ticket, buffers.own.at[:, pl.ds((1 - core) * (KVH // 2), KVH // 2)])
            ahead = copies.start(buffers.own, buffers.back1, place.device("z", 1))
            behind = copies.start(buffers.own, buffers.ahead1, place.device("z", -1))
            edge = copies.start(buffers.own.at[1], buffers.edge, place.along(1))
            yield times[1], []
            copies.arrived(ahead, buffers.back1)
            ahead = copies.start(buffers.back1, buffers.back2, place.device("z", 1))
            copies.arrived(behind, buffers.ahead1)
            behind = copies.start(buffers.ahead1, buffers.ahead2, place.device("z", -1))
            send_slots(buffers, 0, row_tickets)
            yield times[2], []
            copies.arrived(ahead, buffers.back2)
            ahead = send_far(buffers, 1)
            copies.arrived(behind, buffers.ahead2)
            behind = send_far(buffers, -1)
            send_slots(buffers, 1, row_tickets)
            yield times[3], []
            tail = pl.ds(columns, columns // 2)
            copies.arrived(ahead, buffers.far_back)
            ahead = copies.start(buffers.far_back.at[tail], buffers.last.at[0], place.device("z", 1))
            copies.arrived(behind, buffers.far_ahead)
            behind = copies.start(buffers.far_ahead.at[tail], buffers.last.at[1], place.device("z", -1))
            send_slots(buffers, 2, row_tickets)
            yield times[4], []
            copies.arrived(ahead, buffers.last.at[0])
            copies.arrived(behind, buffers.last.at[1])
            send_slots(buffers, 3, row_tickets)
            yield times[5], []
            copies.arrived(edge, buffers.edge)
            for ticket, target in row_tickets:
                copies.arrived(ticket, target)
            yield times[5], then

        return [task()]

    def candidates(kind, block, head):
        buffers = kinds[kind]
        device = lax.div(own_list[0, block * KVH + head], 2)
        distance = lax.rem(lax.div(device, columns) - z + rows_z, rows_z)
        slot = jnp.where(
            distance < 4, 2 * distance, jnp.where(distance == 4, 7, 2 * (rows_z - distance) - 1)
        )
        before = buffers.edge[head] if block == 0 else buffers.own[0, head]
        return jnp.concatenate(
            [buffers.own[block, head], before, buffers.arrived[lax.rem(device, columns), slot]], axis=0
        )

    def weights_task(block, head_range, wake):
        def one_head(head, carry):
            rows = slice(block * BLOCK, (block + 1) * BLOCK)
            query = queries[rows, pl.ds(pl.multiple_of(head * GROUP * DH, GROUP * DH), GROUP * DH)]
            query = jnp.concatenate([query[:, g * DH : (g + 1) * DH] for g in range(GROUP)], axis=0)
            scores = lax.dot_general(
                query, candidates(0, block, head), (((1,), (1,)), ((), ())), preferred_element_type=jnp.float32
            ) * (math.log2(math.e) / math.sqrt(DH))
            if block == 0:
                index = lax.broadcasted_iota(jnp.int32, scores.shape, 1)
                blocked = (place.seq == 0) & (index >= BLOCK) & (index < 2 * BLOCK)
                scores = jnp.where(blocked, -1e30, scores)
            raised = jnp.exp2(scores - jnp.max(scores, axis=-1, keepdims=True))
            scale = 1.0 / jnp.sum(raised, axis=-1, keepdims=True)
            softmax[block * KVH + head] = (raised * scale).astype(jnp.bfloat16)
            return carry

        yield wake, []
        if block == 0 and head_range[0] == 0:
            loads["queries"].wait()
            loads["own_list"].wait()
        lax.fori_loop(*head_range, one_head, 0)

    def output_task():
        yield plan["output"], []
        for block in range(2):

            def one_head(head, carry, block=block):
                result = jnp.dot(
                    softmax[block * KVH + head], candidates(1, block, head), preferred_element_type=jnp.float32
                ).astype(jnp.bfloat16)
                for g in range(GROUP):
                    lanes = pl.ds(pl.multiple_of((head * GROUP + g) * DH, DH), DH)
                    out_ref[block * BLOCK : (block + 1) * BLOCK, lanes] = result[g * BLOCK : (g + 1) * BLOCK]
                return carry

            lax.fori_loop(0, KVH, one_head, 0)

    half = KVH // 2
    both = Group(lambda wake: [output_task()])
    softmax_tasks = [
        both.add(weights_task(block, (begin, begin + half), plan["softmax"][block * 2 + begin // half]))
        for block in range(2) for begin in (0, half)
    ]
    values_ready = both.add(iter(()))
    groups = [
        Group(lambda wake: exchange(0, softmax_tasks)),
        Group(lambda wake: exchange(1, [values_ready])),
    ]
    gathers = [
        gather_weight(place, copies, groups[kind], weights, kind, part, axes, plan["begin"][kind], plan["spans"])
        for kind in range(2) for part, axes in enumerate((("y", "x"), ("x", "y")))
    ]
    tasks = [first_task(gathers), list_task()]
    run_tasks(tasks)
    copies.sent()
    assert len(copies.started) == COPIES, len(copies.started)


PLAN = {
    "first": (0.1, 2.4),
    "lists": ((0.2, 2.4), (14.2, 4.0), 44.5),
    "begin": (10.0, 44.0),
    "spans": (2.0, 5.0, 9.0),
    "exchange": ((43.0, 53.0, 66.0, 79.0, 83.0, 88.0), (74.0, 84.0, 96.0, 107.0, 111.0, 116.0)),
    "softmax": (88.5, 90.5, 97.0, 99.0),
    "output": 117.0,
}


def layer(lists, tokens, queries, key_weight, value_weight, sizes):
    local_tokens, depth = tokens.shape
    part_rows, width = key_weight.shape
    columns, rows = 2 * sizes["y"], sizes["z"]
    hbm = pl.BlockSpec(memory_space=pltpu.HBM)
    kind = Kind.scratch(rows, columns)
    return pl.pallas_call(
        functools.partial(layer_kernel, sizes, PLAN),
        out_shape=jax.ShapeDtypeStruct(queries.shape, jnp.bfloat16),
        in_specs=[hbm] * 5,
        out_specs=pl.BlockSpec(memory_space=pltpu.VMEM),
        scratch_shapes=[
            pltpu.VMEM((2, sizes["x"], rows, sizes["y"], 2 * part_rows, width // 2), jnp.bfloat16),
            pltpu.VMEM((2, local_tokens, depth), jnp.bfloat16),
            pltpu.VMEM(queries.shape, jnp.bfloat16),
            pltpu.VMEM((rows, sizes["y"], 2, 8, LANES), jnp.int32),
            pltpu.VMEM((8, LANES), jnp.int32),
            pltpu.SMEM((8, LANES), jnp.int32),
            pltpu.SMEM((8, LANES), jnp.int32),
            pltpu.VMEM((2 * KVH, GROUP * BLOCK, 3 * BLOCK), jnp.bfloat16),
            *kind,
            *kind,
            pltpu.SemaphoreType.DMA((8,)),
            pltpu.SemaphoreType.DMA((COPIES,)),
            pltpu.SemaphoreType.DMA((COPIES,)),
        ],
        compiler_params=pltpu.CompilerParams(
            collective_id=0, has_side_effects=True, vmem_limit_bytes=58 << 20
        ),
        name="layer",
    )(lists, tokens, queries, key_weight, value_weight)


COPIES = 178


def local(tokens, queries, key_weight, value_weight, sorted_blocks):
    devices = lax.axis_size("seq")
    sizes = {"x": lax.axis_size("fsdp"), "y": 4, "z": devices // 8}
    own = sorted_blocks[0].T.reshape(-1)
    lists = jnp.broadcast_to(jnp.pad(own, (0, LANES - own.shape[0]), constant_values=-1), (8, LANES))
    return layer(lists, tokens[0], queries[0], key_weight, value_weight, sizes)[None]


def solution(mesh):
    placed = (
        P("fsdp", "seq", None),
        P("fsdp", "seq", None),
        P(("fsdp", "seq"), None),
        P(("fsdp", "seq"), None),
        P("fsdp", None, "seq"),
    )
    return jax.shard_map(
        local, mesh=mesh, in_specs=placed, out_specs=P("fsdp", "seq", None), check_vma=False
    )
```

```python
import functools
import math

import jax
import jax.numpy as jnp
from jax import lax
from jax.experimental import pallas as pl
from jax.experimental.pallas import tpu as pltpu
from jax.sharding import PartitionSpec as P

DH = 128
KVH = 8
GROUP = 4
BLOCK = 128
MESH = pl.DeviceIdType.MESH
AXES = ("x", "z", "y")
FULL = slice(None)
LANES = 128
STAGES = (((0, 0), (0, 5), (5, 7), (7, 8)), ((0, 3), (3, 5), (5, 7), (7, 8)))


class Place:
    def __init__(self, sizes):
        self.sizes = sizes
        self.seq = lax.axis_index("seq")
        self.core = lax.rem(self.seq, 2)
        pair = lax.div(self.seq, 2)
        self.at = {"x": lax.axis_index("fsdp"), "y": lax.rem(pair, sizes["y"]), "z": lax.div(pair, sizes["y"])}
        self.columns = 2 * sizes["y"]
        self.column = self.at["y"] * 2 + self.core

    def moved(self, axis, steps):
        return lax.rem(self.at[axis] + (steps % self.sizes[axis]), self.sizes[axis])

    def device(self, axis, steps):
        at = dict(self.at)
        at[axis] = self.moved(axis, steps)
        return (at["x"], (at["z"] * self.sizes["y"] + at["y"]) * 2 + self.core)

    def sibling(self):
        return (self.at["x"], self.at["z"] * self.columns + self.at["y"] * 2 + 1 - self.core)

    def other_column(self, steps):
        return lax.rem(self.column + (steps % self.columns), self.columns)

    def in_row(self, steps):
        return (self.at["x"], self.at["z"] * self.columns + self.other_column(steps))

    def along(self, steps):
        count = self.sizes["z"] * self.columns
        return (self.at["x"], lax.rem(self.seq + (steps % count), count))


class Copies:
    def __init__(self, send_sem, recv_sem):
        self.send_sem, self.recv_sem = send_sem, recv_sem
        self.started = []

    def make(self, slot, source, target, device):
        return pltpu.make_async_remote_copy(
            src_ref=source, dst_ref=target, send_sem=self.send_sem.at[slot], recv_sem=self.recv_sem.at[slot],
            device_id=device, device_id_type=MESH,
        )

    def start(self, source, target, device):
        slot = len(self.started)
        copy = self.make(slot, source, target, device)
        copy.start()
        self.started.append(copy)
        return slot, device

    def arrived(self, ticket, target):
        self.make(ticket[0], target, target, ticket[1]).wait_recv()

    def sent(self):
        for copy in self.started:
            copy.wait_send()


def run_tasks(tasks):
    count = 0
    queue = []
    for task in tasks:
        queue.append([0.0, count, task])
        count += 1
    while queue:
        queue.sort(key=lambda entry: entry[:2])
        entry = queue[0]
        try:
            wake, more = next(entry[2])
            entry[0] = wake
            for task in more:
                queue.append([wake, count, task])
                count += 1
        except StopIteration:
            queue.pop(0)


class Group:
    def __init__(self, then):
        self.open, self.then = 0, then

    def add(self, task):
        self.open += 1

        def run():
            wake = 0.0
            for wake, more in task:
                yield wake, more
            self.open -= 1
            if self.open == 0:
                yield wake, self.then(wake)

        return run()


def ring(place, copies, piece, axis, where, begin, span, on_arrival, halves=True):
    half_way = place.sizes[axis] // 2
    yield begin, []
    own = piece({**where, axis: place.at[axis]}, None)
    ahead = copies.start(own, own, place.device(axis, 1))
    behind = copies.start(own, own, place.device(axis, -1))
    for step in range(1, half_way + 1):
        last, split = step == half_way, step + 1 == half_way
        before = {**where, axis: place.moved(axis, -step)}
        after = {**where, axis: place.moved(axis, step)}
        time = begin + step * span
        yield time, []
        copies.arrived(ahead, piece(before, 0 if last and halves else None))
        if not last:
            ref = piece(before, 0 if split and halves else None)
            ahead = copies.start(ref, ref, place.device(axis, 1))
        if not last or halves:
            copies.arrived(behind, piece(after, 1 if last else None))
        if not last and not (split and not halves):
            ref = piece(after, 1 if split else None)
            behind = copies.start(ref, ref, place.device(axis, -1))
        for here in [after] if last else [before, after]:
            more = on_arrival(here, time)
            if more:
                yield time, more


def gather_weight(place, copies, group, weights, kind, part, axes, begin, spans):
    second, third = axes
    width = weights.shape[-1] // 2

    def piece(where, half):
        rows = FULL if half is None else pl.ds(half * 16, 16)
        return weights.at[kind, where["x"], :, where["y"], rows, pl.ds(part * width, width)]

    def nothing(here, time):
        return []

    def third_ring(where, time):
        return group.add(ring(place, copies, piece, third, {**where, third: place.at[third]}, time, spans[2], nothing))

    def whole():
        yield begin, [
            group.add(ring(place, copies, piece, second, dict(place.at), begin, spans[1], lambda here, time: [third_ring(here, time)])),
            third_ring(dict(place.at), begin),
        ]

    return group.add(whole())


class Kind:
    names = ("own", "back1", "ahead1", "back2", "ahead2", "swap", "edge", "far_out", "far_back", "far_ahead", "last", "slots", "arrived")

    def __init__(self, refs):
        for name, ref in zip(self.names, refs):
            setattr(self, name, ref)

    @classmethod
    def scratch(cls, rows, columns):
        half = KVH // 2
        block = (BLOCK, DH)
        shapes = [(2, KVH)] * 5 + [(2, half), (KVH,), (2, columns + columns // 2)]
        shapes += [(columns + columns // 2,)] * 2 + [(2, columns // 2), (columns - 1, rows), (columns, rows)]
        return [pltpu.VMEM(shape + block, jnp.bfloat16) for shape in shapes]


def layer_kernel(sizes, plan, list_ref, tokens_ref, queries_ref, key_ref, value_ref, out_ref,
                 weights, tokens, queries, lists, wanted_vector, wanted, own_list, softmax, partial, *rest):
    kinds = [Kind(rest[:13]), Kind(rest[13:26])]
    load_sem, send_sem, recv_sem = rest[26:]
    place = Place(sizes)
    copies = Copies(send_sem, recv_sem)
    x, z, y, core = place.at["x"], place.at["z"], place.at["y"], place.core
    columns, rows_z = place.columns, sizes["z"]
    half_width = key_ref.shape[1] // 2
    part_width = half_width // 2

    loads = {}

    def load(name, source, target):
        loads[name] = pltpu.make_async_copy(source, target, load_sem.at[len(loads)])
        loads[name].start()

    def weight_columns(ref, which):
        return ref.at[:, pl.ds(pl.multiple_of(which * half_width, half_width), half_width)]

    def weight_rows(kind, which):
        return weights.at[kind, x, z, y, pl.ds(which * 16, 16), :]

    weight_refs = (key_ref, value_ref)
    for kind in range(2):
        load(kind, weight_columns(weight_refs[kind], core), weight_rows(kind, core))
    load("own_list", list_ref, own_list)
    load("lists", list_ref, lists.at[z, y, core])
    load("tokens", tokens_ref, tokens.at[core])
    load("queries", queries_ref, queries)

    barrier = pltpu.get_barrier_semaphore()
    peers = [place.device(axis, step) for axis in ("x", "z") for step in (1, -1)]
    peers += [place.in_row(step) for step in range(1, columns)]
    peers += [place.along(1), place.along(-1)]
    for device in peers:
        pl.semaphore_signal(barrier, inc=1, device_id=device, device_id_type=MESH)
    pl.semaphore_wait(barrier, len(peers))

    shared = {}
    for kind in range(2):
        shared[kind] = copies.start(
            weight_columns(weight_refs[kind], 1 - core), weight_rows(kind, core), place.sibling()
        )

    def first_task(then):
        for kind in range(2):
            loads[kind].wait()
            copies.arrived(shared[kind], weight_rows(kind, 1 - core))

        def piece(where, half):
            rows = FULL if half is None else pl.ds(half * 16, 16)
            return weights.at[:, where["x"], where["z"], where["y"], rows, :]

        yield from ring(place, copies, piece, "z", dict(place.at), *plan["first"], lambda here, time: [])
        shared["tokens"] = copies.start(tokens_ref, tokens.at[core], place.sibling())
        yield plan["first"][0] + 4 * plan["first"][1], then

    def list_task():
        def piece(where, half):
            return lists.at[where["z"], where["y"], core]

        def nothing(here, time):
            return []

        loads["lists"].wait()
        yield from ring(place, copies, piece, "z", dict(place.at), *plan["lists"][0], nothing, halves=False)
        yield from ring(place, copies, piece, "y", {**place.at, "z": FULL}, *plan["lists"][1], nothing, halves=False)
        mine = lists.at[:, :, core]
        ticket = copies.start(mine, mine, place.sibling())
        yield plan["lists"][2], []
        copies.arrived(ticket, lists.at[:, :, 1 - core])
        lane = lax.broadcasted_iota(jnp.int32, (8, LANES), 1)
        source = lax.broadcasted_iota(jnp.int32, (8, LANES), 0) * columns + place.column

        def one_device(device, total):
            tile = lists[lax.div(device, columns), lax.div(lax.rem(device, columns), 2), lax.rem(device, 2)]
            item = (tile & 1) * KVH + (lane & 7) + 1
            found = jnp.sum(jnp.where((tile >> 1) == source, item, 0), axis=1, keepdims=True)
            return jnp.where(lane == device, found, total)

        wanted_vector[...] = lax.fori_loop(0, rows_z * columns, one_device, jnp.zeros((8, LANES), jnp.int32), unroll=8)
        copy = pltpu.make_async_copy(wanted_vector, wanted, load_sem.at[len(loads)])
        copy.start()
        copy.wait()

    def picked(ref, steps, row_steps, column):
        device = place.moved("z", row_steps) * columns + column
        item = jnp.clip(wanted[place.moved("z", steps), device] - 1, 0, 2 * KVH - 1)
        return ref[lax.div(item, KVH), lax.rem(item, KVH)]

    def project(kind):
        buffers = kinds[kind]
        if kind == 0:
            loads["tokens"].wait()
            copies.arrived(shared["tokens"], tokens.at[1 - core])
        for part in range(2):
            weight = weights[kind, :, :, :, :, part * part_width : (part + 1) * part_width].reshape(tokens.shape[2], part_width)
            for mine in (False, True):
                which = core if mine else 1 - core
                result = jnp.dot(tokens[which], weight, preferred_element_type=jnp.float32).astype(jnp.bfloat16)
                for block in range(2):
                    for head in range(2):
                        value = result[block * BLOCK : (block + 1) * BLOCK, head * DH : (head + 1) * DH]
                        if mine:
                            buffers.own[block, core * (KVH // 2) + part * 2 + head] = value
                        else:
                            buffers.swap[block, part * 2 + head] = value
        return copies.start(buffers.swap, buffers.own.at[:, pl.ds(core * (KVH // 2), KVH // 2)], place.sibling())

    def send_slots(kind, stage, row_tickets):
        buffers = kinds[kind]
        begin, end = STAGES[kind][stage]
        if begin == end:
            return
        sources = {0: (buffers.own, 0), 1: (buffers.back1, -1), 2: (buffers.ahead1, 1), 3: (buffers.back2, -2), 4: (buffers.ahead2, 2)}

        def value(slot, column):
            if slot < 5:
                return picked(*sources[slot], 0, column)
            if slot == 5:
                return buffers.far_back[column]
            if slot == 6:
                return buffers.far_ahead[column]
            return buffers.last[lax.rem(column, 2), lax.div(column, 2)]

        for slot in range(begin, end):
            buffers.arrived[place.column, slot] = value(slot, place.column)
        for step in range(1, columns):
            column = place.other_column(step)
            for slot in range(begin, end):
                buffers.slots[step - 1, slot] = value(slot, column)
            ticket = copies.start(
                buffers.slots.at[step - 1, pl.ds(begin, end - begin)],
                buffers.arrived.at[place.column, pl.ds(begin, end - begin)],
                place.in_row(step),
            )
            row_tickets.append((ticket, buffers.arrived.at[place.other_column(-step), pl.ds(begin, end - begin)]))

    def send_far(buffers, direction):
        ref = buffers.back2 if direction == 1 else buffers.ahead2
        side = 0 if direction == 1 else 1
        for column in range(columns):
            buffers.far_out[side, column] = picked(ref, -2 * direction, direction, column)
        for index in range(columns // 2):
            buffers.far_out[side, columns + index] = picked(ref, -2 * direction, 2 * direction, 2 * index + side)
        target = buffers.far_back if direction == 1 else buffers.far_ahead
        return copies.start(buffers.far_out.at[side], target, place.device("z", direction))

    def exchange(kind, then):
        times = plan["exchange"][kind]

        def task():
            buffers = kinds[kind]
            row_tickets = []
            ticket = project(kind)
            yield times[0], []
            copies.arrived(ticket, buffers.own.at[:, pl.ds((1 - core) * (KVH // 2), KVH // 2)])
            ahead = copies.start(buffers.own, buffers.back1, place.device("z", 1))
            behind = copies.start(buffers.own, buffers.ahead1, place.device("z", -1))
            edge = copies.start(buffers.own.at[1], buffers.edge, place.along(1))
            yield times[1], []
            copies.arrived(ahead, buffers.back1)
            ahead = copies.start(buffers.back1, buffers.back2, place.device("z", 1))
            copies.arrived(behind, buffers.ahead1)
            behind = copies.start(buffers.ahead1, buffers.ahead2, place.device("z", -1))
            send_slots(kind, 0, row_tickets)
            yield times[2], []
            copies.arrived(ahead, buffers.back2)
            ahead = send_far(buffers, 1)
            copies.arrived(behind, buffers.ahead2)
            behind = send_far(buffers, -1)
            send_slots(kind, 1, row_tickets)
            yield times[3], []
            tail = pl.ds(columns, columns // 2)
            copies.arrived(ahead, buffers.far_back)
            ahead = copies.start(buffers.far_back.at[tail], buffers.last.at[0], place.device("z", 1))
            copies.arrived(behind, buffers.far_ahead)
            behind = copies.start(buffers.far_ahead.at[tail], buffers.last.at[1], place.device("z", -1))
            send_slots(kind, 2, row_tickets)
            yield times[4], []
            copies.arrived(ahead, buffers.last.at[0])
            copies.arrived(behind, buffers.last.at[1])
            send_slots(kind, 3, row_tickets)
            if kind == 1:
                copies.arrived(edge, buffers.edge)
                partial_output()
            yield times[5], []
            if kind == 0:
                copies.arrived(edge, buffers.edge)
            for ticket, target in row_tickets:
                copies.arrived(ticket, target)
            yield times[5], then

        return [task()]

    def near_pair(kind, block, head):
        buffers = kinds[kind]
        before = buffers.edge[head] if block == 0 else buffers.own[0, head]
        return [buffers.own[block, head], before]

    def chosen(kind, block, head):
        device = lax.div(own_list[0, block * KVH + head], 2)
        distance = lax.rem(lax.div(device, columns) - z + rows_z, rows_z)
        slot = jnp.where(
            distance < 4, 2 * distance, jnp.where(distance == 4, 7, 2 * (rows_z - distance) - 1)
        )
        return kinds[kind].arrived[lax.rem(device, columns), slot]

    def weights_task(block, head_range, wake):
        def one_head(head, carry):
            rows = slice(block * BLOCK, (block + 1) * BLOCK)
            query = queries[rows, pl.ds(pl.multiple_of(head * GROUP * DH, GROUP * DH), GROUP * DH)]
            query = jnp.concatenate([query[:, g * DH : (g + 1) * DH] for g in range(GROUP)], axis=0)
            scores = lax.dot_general(
                query, jnp.concatenate(near_pair(0, block, head) + [chosen(0, block, head)], axis=0), (((1,), (1,)), ((), ())), preferred_element_type=jnp.float32
            ) * (math.log2(math.e) / math.sqrt(DH))
            if block == 0:
                index = lax.broadcasted_iota(jnp.int32, scores.shape, 1)
                blocked = (place.seq == 0) & (index >= BLOCK) & (index < 2 * BLOCK)
                scores = jnp.where(blocked, -1e30, scores)
            raised = jnp.exp2(scores - jnp.max(scores, axis=-1, keepdims=True))
            scale = 1.0 / jnp.sum(raised, axis=-1, keepdims=True)
            softmax[block * KVH + head] = (raised * scale).astype(jnp.bfloat16)
            return carry

        yield wake, []
        if block == 0 and head_range[0] == 0:
            loads["queries"].wait()
            loads["own_list"].wait()
        lax.fori_loop(*head_range, one_head, 0)

    def partial_output():
        for block in range(2):

            def one_head(head, carry, block=block):
                item = block * KVH + head
                partial[item] = jnp.dot(
                    softmax[item, :, : 2 * BLOCK], jnp.concatenate(near_pair(1, block, head), axis=0),
                    preferred_element_type=jnp.float32,
                )
                return carry

            lax.fori_loop(0, KVH, one_head, 0)

    def output_task():
        yield plan["output"], []
        for block in range(2):

            def one_head(head, carry, block=block):
                item = block * KVH + head
                result = partial[item] + jnp.dot(
                    softmax[item, :, 2 * BLOCK :], chosen(1, block, head), preferred_element_type=jnp.float32
                )
                result = result.astype(jnp.bfloat16)
                for g in range(GROUP):
                    lanes = pl.ds(pl.multiple_of((head * GROUP + g) * DH, DH), DH)
                    out_ref[block * BLOCK : (block + 1) * BLOCK, lanes] = result[g * BLOCK : (g + 1) * BLOCK]
                return carry

            lax.fori_loop(0, KVH, one_head, 0)

    half = KVH // 2
    both = Group(lambda wake: [output_task()])
    softmax_tasks = [
        both.add(weights_task(block, (begin, begin + half), plan["softmax"][block * 2 + begin // half]))
        for block in range(2) for begin in (0, half)
    ]
    values_ready = both.add(iter(()))
    groups = [
        Group(lambda wake: exchange(0, softmax_tasks)),
        Group(lambda wake: exchange(1, [values_ready])),
    ]
    gathers = [
        gather_weight(place, copies, groups[kind], weights, kind, part, axes, plan["begin"][kind], plan["spans"])
        for kind in range(2) for part, axes in enumerate((("y", "x"), ("x", "y")))
    ]
    tasks = [first_task(gathers), list_task()]
    run_tasks(tasks)
    copies.sent()
    assert len(copies.started) == COPIES, len(copies.started)


PLAN = {
    "first": (0.1, 2.4),
    "lists": ((0.2, 2.4), (14.2, 4.0), 44.5),
    "begin": (10.0, 44.0),
    "spans": (2.0, 5.0, 9.0),
    "exchange": ((43.0, 53.0, 66.0, 79.0, 83.0, 88.0), (74.0, 84.0, 96.0, 107.0, 111.0, 116.0)),
    "softmax": (88.5, 90.5, 97.0, 99.0),
    "output": 117.0,
}


def layer(lists, tokens, queries, key_weight, value_weight, sizes):
    local_tokens, depth = tokens.shape
    part_rows, width = key_weight.shape
    columns, rows = 2 * sizes["y"], sizes["z"]
    hbm = pl.BlockSpec(memory_space=pltpu.HBM)
    kind = Kind.scratch(rows, columns)
    return pl.pallas_call(
        functools.partial(layer_kernel, sizes, PLAN),
        out_shape=jax.ShapeDtypeStruct(queries.shape, jnp.bfloat16),
        in_specs=[hbm] * 5,
        out_specs=pl.BlockSpec(memory_space=pltpu.VMEM),
        scratch_shapes=[
            pltpu.VMEM((2, sizes["x"], rows, sizes["y"], 2 * part_rows, width // 2), jnp.bfloat16),
            pltpu.VMEM((2, local_tokens, depth), jnp.bfloat16),
            pltpu.VMEM(queries.shape, jnp.bfloat16),
            pltpu.VMEM((rows, sizes["y"], 2, 8, LANES), jnp.int32),
            pltpu.VMEM((8, LANES), jnp.int32),
            pltpu.SMEM((8, LANES), jnp.int32),
            pltpu.SMEM((8, LANES), jnp.int32),
            pltpu.VMEM((2 * KVH, GROUP * BLOCK, 3 * BLOCK), jnp.bfloat16),
            pltpu.VMEM((2 * KVH, GROUP * BLOCK, DH), jnp.float32),
            *kind,
            *kind,
            pltpu.SemaphoreType.DMA((8,)),
            pltpu.SemaphoreType.DMA((COPIES,)),
            pltpu.SemaphoreType.DMA((COPIES,)),
        ],
        compiler_params=pltpu.CompilerParams(
            collective_id=0, has_side_effects=True, vmem_limit_bytes=58 << 20
        ),
        name="layer",
    )(lists, tokens, queries, key_weight, value_weight)


COPIES = 171


def local(tokens, queries, key_weight, value_weight, sorted_blocks):
    devices = lax.axis_size("seq")
    sizes = {"x": lax.axis_size("fsdp"), "y": 4, "z": devices // 8}
    own = sorted_blocks[0].T.reshape(-1)
    lists = jnp.broadcast_to(jnp.pad(own, (0, LANES - own.shape[0]), constant_values=-1), (8, LANES))
    return layer(lists, tokens[0], queries[0], key_weight, value_weight, sizes)[None]


def solution(mesh):
    placed = (
        P("fsdp", "seq", None),
        P("fsdp", "seq", None),
        P(("fsdp", "seq"), None),
        P(("fsdp", "seq"), None),
        P("fsdp", None, "seq"),
    )
    return jax.shard_map(
        local, mesh=mesh, in_specs=placed, out_specs=P("fsdp", "seq", None), check_vma=False
    )
```

```python
import functools
import math

import jax
import jax.numpy as jnp
from jax import lax
from jax.experimental import pallas as pl
from jax.experimental.pallas import tpu as pltpu
from jax.sharding import PartitionSpec as P

DH = 128
KVH = 8
GROUP = 4
BLOCK = 128
MESH = pl.DeviceIdType.MESH
AXES = ("x", "z", "y")
FULL = slice(None)
LANES = 128
HALF_HOP = 5.0
STAGES = (((0, 0), (0, 0), (0, 7), (7, 8)), ((0, 3), (3, 5), (5, 7), (7, 8)))


class Place:
    def __init__(self, sizes):
        self.sizes = sizes
        self.seq = lax.axis_index("seq")
        self.core = lax.rem(self.seq, 2)
        pair = lax.div(self.seq, 2)
        self.at = {"x": lax.axis_index("fsdp"), "y": lax.rem(pair, sizes["y"]), "z": lax.div(pair, sizes["y"])}
        self.columns = 2 * sizes["y"]
        self.column = self.at["y"] * 2 + self.core

    def moved(self, axis, steps):
        return lax.rem(self.at[axis] + (steps % self.sizes[axis]), self.sizes[axis])

    def device(self, axis, steps):
        at = dict(self.at)
        at[axis] = self.moved(axis, steps)
        return (at["x"], (at["z"] * self.sizes["y"] + at["y"]) * 2 + self.core)

    def sibling(self):
        return (self.at["x"], self.at["z"] * self.columns + self.at["y"] * 2 + 1 - self.core)

    def other_column(self, steps):
        return lax.rem(self.column + (steps % self.columns), self.columns)

    def in_row(self, steps):
        return (self.at["x"], self.at["z"] * self.columns + self.other_column(steps))

    def along(self, steps):
        count = self.sizes["z"] * self.columns
        return (self.at["x"], lax.rem(self.seq + (steps % count), count))


class Copies:
    def __init__(self, send_sem, recv_sem):
        self.send_sem, self.recv_sem = send_sem, recv_sem
        self.started = []

    def make(self, slot, source, target, device):
        return pltpu.make_async_remote_copy(
            src_ref=source, dst_ref=target, send_sem=self.send_sem.at[slot], recv_sem=self.recv_sem.at[slot],
            device_id=device, device_id_type=MESH,
        )

    def start(self, source, target, device):
        slot = len(self.started)
        copy = self.make(slot, source, target, device)
        copy.start()
        self.started.append(copy)
        return slot, device

    def arrived(self, ticket, target):
        self.make(ticket[0], target, target, ticket[1]).wait_recv()

    def sent(self):
        for copy in self.started:
            copy.wait_send()


def run_tasks(tasks):
    count = 0
    queue = []
    for task in tasks:
        queue.append([0.0, count, task])
        count += 1
    while queue:
        queue.sort(key=lambda entry: entry[:2])
        entry = queue[0]
        try:
            wake, more = next(entry[2])
            entry[0] = wake
            for task in more:
                queue.append([wake, count, task])
                count += 1
        except StopIteration:
            queue.pop(0)


class Group:
    def __init__(self, then):
        self.open, self.then = 0, then

    def add(self, task):
        self.open += 1

        def run():
            wake = 0.0
            for wake, more in task:
                yield wake, more
            self.open -= 1
            if self.open == 0:
                yield wake, self.then(wake)

        return run()


def ring(place, copies, piece, axis, where, begin, span, on_arrival, halves=True):
    half_way = place.sizes[axis] // 2
    yield begin, []
    own = piece({**where, axis: place.at[axis]}, None)
    ahead = copies.start(own, own, place.device(axis, 1))
    behind = copies.start(own, own, place.device(axis, -1))
    for step in range(1, half_way + 1):
        last, split = step == half_way, step + 1 == half_way
        before = {**where, axis: place.moved(axis, -step)}
        after = {**where, axis: place.moved(axis, step)}
        time = begin + step * span
        yield time, []
        copies.arrived(ahead, piece(before, 0 if last and halves else None))
        if not last:
            ref = piece(before, 0 if split and halves else None)
            ahead = copies.start(ref, ref, place.device(axis, 1))
        if not last or halves:
            copies.arrived(behind, piece(after, 1 if last else None))
        if not last and not (split and not halves):
            ref = piece(after, 1 if split else None)
            behind = copies.start(ref, ref, place.device(axis, -1))
        for here in [after] if last else [before, after]:
            more = on_arrival(here, time)
            if more:
                yield time, more


def gather_weight(place, copies, group, weights, kind, part, axes, begin, spans):
    second, third = axes
    width = weights.shape[-1] // 2

    def piece(where, half):
        rows = FULL if half is None else pl.ds(half * 16, 16)
        return weights.at[kind, where["x"], :, where["y"], rows, pl.ds(part * width, width)]

    def nothing(here, time):
        return []

    def third_ring(where, time):
        return group.add(ring(place, copies, piece, third, {**where, third: place.at[third]}, time, spans[2], nothing))

    def whole():
        yield begin, [
            group.add(ring(place, copies, piece, second, dict(place.at), begin, spans[1], lambda here, time: [third_ring(here, time)])),
            third_ring(dict(place.at), begin),
        ]

    return group.add(whole())


class Kind:
    names = ("own", "back1", "ahead1", "back2", "ahead2", "swap", "edge", "far_out", "far_back", "far_ahead", "last", "slots", "arrived")

    def __init__(self, refs):
        for name, ref in zip(self.names, refs):
            setattr(self, name, ref)

    @classmethod
    def scratch(cls, rows, columns):
        half = KVH // 2
        block = (BLOCK, DH)
        shapes = [(2, KVH)] * 5 + [(2, half), (KVH,), (2, columns + columns // 2)]
        shapes += [(columns + columns // 2,)] * 2 + [(2, columns // 2), (columns - 1, rows), (columns, rows)]
        return [pltpu.VMEM(shape + block, jnp.bfloat16) for shape in shapes]


def layer_kernel(sizes, plan, list_ref, tokens_ref, queries_ref, key_ref, value_ref, out_ref,
                 weights, tokens, queries, lists, wanted_vector, wanted, own_list, softmax, partial, *rest):
    kinds = [Kind(rest[:13]), Kind(rest[13:26])]
    load_sem, send_sem, recv_sem = rest[26:]
    place = Place(sizes)
    copies = Copies(send_sem, recv_sem)
    x, z, y, core = place.at["x"], place.at["z"], place.at["y"], place.core
    columns, rows_z = place.columns, sizes["z"]
    half_width = key_ref.shape[1] // 2
    part_width = half_width // 2

    loads = {}

    def load(name, source, target):
        loads[name] = pltpu.make_async_copy(source, target, load_sem.at[len(loads)])
        loads[name].start()

    def weight_columns(ref, which):
        return ref.at[:, pl.ds(pl.multiple_of(which * half_width, half_width), half_width)]

    def weight_rows(kind, which):
        return weights.at[kind, x, z, y, pl.ds(which * 16, 16), :]

    weight_refs = (key_ref, value_ref)
    for kind in range(2):
        load(kind, weight_columns(weight_refs[kind], core), weight_rows(kind, core))
    load("own_list", list_ref, own_list)
    load("lists", list_ref, lists.at[z, y, core])
    load("tokens", tokens_ref, tokens.at[core])
    load("queries", queries_ref, queries)

    barrier = pltpu.get_barrier_semaphore()
    peers = [place.device(axis, step) for axis in ("x", "z") for step in (1, -1)]
    peers += [place.in_row(step) for step in range(1, columns)]
    peers += [place.along(1), place.along(-1)]
    for device in peers:
        pl.semaphore_signal(barrier, inc=1, device_id=device, device_id_type=MESH)
    pl.semaphore_wait(barrier, len(peers))

    shared = {}
    for kind in range(2):
        shared[kind] = copies.start(
            weight_columns(weight_refs[kind], 1 - core), weight_rows(kind, core), place.sibling()
        )

    def first_task(kind, then):
        begin, span = plan["first"][kind]
        yield begin, []
        loads[kind].wait()
        copies.arrived(shared[kind], weight_rows(kind, 1 - core))

        def piece(where, half):
            rows = FULL if half is None else pl.ds(half * 16, 16)
            return weights.at[kind, where["x"], where["z"], where["y"], rows, :]

        yield from ring(place, copies, piece, "z", dict(place.at), begin, span, lambda here, time: [])
        if kind == 0:
            shared["tokens"] = copies.start(tokens_ref, tokens.at[core], place.sibling())
        yield begin + 4 * span, then

    def list_task():
        def piece(where, half):
            return lists.at[where["z"], where["y"], core]

        def nothing(here, time):
            return []

        loads["lists"].wait()
        yield from ring(place, copies, piece, "z", dict(place.at), *plan["lists"][0], nothing, halves=False)
        yield from ring(place, copies, piece, "y", {**place.at, "z": FULL}, *plan["lists"][1], nothing, halves=False)
        mine = lists.at[:, :, core]
        ticket = copies.start(mine, mine, place.sibling())
        yield plan["lists"][2], []
        copies.arrived(ticket, lists.at[:, :, 1 - core])
        lane = lax.broadcasted_iota(jnp.int32, (8, LANES), 1)
        source = lax.broadcasted_iota(jnp.int32, (8, LANES), 0) * columns + place.column

        def one_device(device, total):
            tile = lists[lax.div(device, columns), lax.div(lax.rem(device, columns), 2), lax.rem(device, 2)]
            item = (tile & 1) * KVH + (lane & 7) + 1
            found = jnp.sum(jnp.where((tile >> 1) == source, item, 0), axis=1, keepdims=True)
            return jnp.where(lane == device, found, total)

        wanted_vector[...] = lax.fori_loop(0, rows_z * columns, one_device, jnp.zeros((8, LANES), jnp.int32), unroll=8)
        copy = pltpu.make_async_copy(wanted_vector, wanted, load_sem.at[len(loads)])
        copy.start()
        copy.wait()

    def picked(ref, steps, row_steps, column):
        device = place.moved("z", row_steps) * columns + column
        item = jnp.clip(wanted[place.moved("z", steps), device] - 1, 0, 2 * KVH - 1)
        return ref[lax.div(item, KVH), lax.rem(item, KVH)]

    def project(kind):
        buffers = kinds[kind]
        if kind == 0:
            loads["tokens"].wait()
            copies.arrived(shared["tokens"], tokens.at[1 - core])
        for mine in (False, True):
            for part in range(2):
                weight = weights[kind, :, :, :, :, part * part_width : (part + 1) * part_width]
                result = jnp.dot(
                    tokens[core if mine else 1 - core], weight.reshape(tokens.shape[2], part_width),
                    preferred_element_type=jnp.float32,
                ).astype(jnp.bfloat16)
                for block in range(2):
                    for head in range(2):
                        value = result[block * BLOCK : (block + 1) * BLOCK, head * DH : (head + 1) * DH]
                        if mine:
                            buffers.own[block, core * (KVH // 2) + part * 2 + head] = value
                        else:
                            buffers.swap[block, part * 2 + head] = value
            if not mine:
                ticket = copies.start(
                    buffers.swap, buffers.own.at[:, pl.ds(core * (KVH // 2), KVH // 2)], place.sibling()
                )
        return ticket

    def send_slots(kind, stage, row_tickets):
        buffers = kinds[kind]
        begin, end = STAGES[kind][stage]
        if begin == end:
            return
        sources = {0: (buffers.own, 0), 1: (buffers.back1, -1), 2: (buffers.ahead1, 1), 3: (buffers.back2, -2), 4: (buffers.ahead2, 2)}

        def value(slot, column):
            if slot < 5:
                return picked(*sources[slot], 0, column)
            if slot == 5:
                return buffers.far_back[column]
            if slot == 6:
                return buffers.far_ahead[column]
            return buffers.last[lax.rem(column, 2), lax.div(column, 2)]

        for slot in range(begin, end):
            buffers.arrived[place.column, slot] = value(slot, place.column)
        for step in range(1, columns):
            column = place.other_column(step)
            for slot in range(begin, end):
                buffers.slots[step - 1, slot] = value(slot, column)
            ticket = copies.start(
                buffers.slots.at[step - 1, pl.ds(begin, end - begin)],
                buffers.arrived.at[place.column, pl.ds(begin, end - begin)],
                place.in_row(step),
            )
            row_tickets.append((ticket, buffers.arrived.at[place.other_column(-step), pl.ds(begin, end - begin)]))

    def send_far(buffers, direction):
        ref = buffers.back2 if direction == 1 else buffers.ahead2
        side = 0 if direction == 1 else 1
        for column in range(columns):
            buffers.far_out[side, column] = picked(ref, -2 * direction, direction, column)
        for index in range(columns // 2):
            buffers.far_out[side, columns + index] = picked(ref, -2 * direction, 2 * direction, 2 * index + side)
        target = buffers.far_back if direction == 1 else buffers.far_ahead
        return copies.start(buffers.far_out.at[side], target, place.device("z", direction))

    def exchange(kind, then):
        times = plan["exchange"][kind]

        def task():
            buffers = kinds[kind]
            row_tickets = []
            ticket = project(kind)
            sides = [pl.ds(core * (KVH // 2), KVH // 2), pl.ds((1 - core) * (KVH // 2), KVH // 2)]
            hops = ((buffers.own, buffers.back1, buffers.back2, 1), (buffers.own, buffers.ahead1, buffers.ahead2, -1))
            first_hop, second_hop = [], []
            for side in range(2):
                if side == 1:
                    yield times[0], []
                    copies.arrived(ticket, buffers.own.at[:, sides[1]])
                for source, near, _, direction in hops:
                    ticket_near = copies.start(source.at[:, sides[side]], near.at[:, sides[side]], place.device("z", direction))
                    first_hop.append(ticket_near)
            edge = copies.start(buffers.own.at[1], buffers.edge, place.along(1))
            for side in range(2):
                yield times[1] - (HALF_HOP if side == 0 else 0.0), []
                for index, (_, near, far, direction) in enumerate(hops):
                    copies.arrived(first_hop[side * 2 + index], near.at[:, sides[side]])
                    second_hop.append(
                        copies.start(near.at[:, sides[side]], far.at[:, sides[side]], place.device("z", direction))
                    )
            send_slots(kind, 0, row_tickets)
            yield times[2], []
            for side in range(2):
                copies.arrived(second_hop[side * 2], buffers.back2.at[:, sides[side]])
            ahead = send_far(buffers, 1)
            for side in range(2):
                copies.arrived(second_hop[side * 2 + 1], buffers.ahead2.at[:, sides[side]])
            behind = send_far(buffers, -1)
            send_slots(kind, 1, row_tickets)
            yield times[3], []
            tail = pl.ds(columns, columns // 2)
            copies.arrived(ahead, buffers.far_back)
            ahead = copies.start(buffers.far_back.at[tail], buffers.last.at[0], place.device("z", 1))
            copies.arrived(behind, buffers.far_ahead)
            behind = copies.start(buffers.far_ahead.at[tail], buffers.last.at[1], place.device("z", -1))
            send_slots(kind, 2, row_tickets)
            yield times[4], []
            copies.arrived(ahead, buffers.last.at[0])
            copies.arrived(behind, buffers.last.at[1])
            send_slots(kind, 3, row_tickets)
            if kind == 1:
                copies.arrived(edge, buffers.edge)
                partial_output()
            yield times[5], []
            if kind == 0:
                copies.arrived(edge, buffers.edge)
            for ticket, target in row_tickets:
                copies.arrived(ticket, target)
            yield times[5], then

        return [task()]

    def near_pair(kind, block, head):
        buffers = kinds[kind]
        before = buffers.edge[head] if block == 0 else buffers.own[0, head]
        return [buffers.own[block, head], before]

    def chosen(kind, block, head):
        device = lax.div(own_list[0, block * KVH + head], 2)
        distance = lax.rem(lax.div(device, columns) - z + rows_z, rows_z)
        slot = jnp.where(
            distance < 4, 2 * distance, jnp.where(distance == 4, 7, 2 * (rows_z - distance) - 1)
        )
        return kinds[kind].arrived[lax.rem(device, columns), slot]

    def weights_task(block, head_range, wake):
        def one_head(head, carry):
            rows = slice(block * BLOCK, (block + 1) * BLOCK)
            query = queries[rows, pl.ds(pl.multiple_of(head * GROUP * DH, GROUP * DH), GROUP * DH)]
            query = jnp.concatenate([query[:, g * DH : (g + 1) * DH] for g in range(GROUP)], axis=0)
            scores = lax.dot_general(
                query, jnp.concatenate(near_pair(0, block, head) + [chosen(0, block, head)], axis=0), (((1,), (1,)), ((), ())), preferred_element_type=jnp.float32
            ) * (math.log2(math.e) / math.sqrt(DH))
            if block == 0:
                index = lax.broadcasted_iota(jnp.int32, scores.shape, 1)
                blocked = (place.seq == 0) & (index >= BLOCK) & (index < 2 * BLOCK)
                scores = jnp.where(blocked, -1e30, scores)
            raised = jnp.exp2(scores - jnp.max(scores, axis=-1, keepdims=True))
            scale = 1.0 / jnp.sum(raised, axis=-1, keepdims=True)
            softmax[block * KVH + head] = (raised * scale).astype(jnp.bfloat16)
            return carry

        yield wake, []
        if block == 0 and head_range[0] == 0:
            loads["queries"].wait()
            loads["own_list"].wait()
        lax.fori_loop(*head_range, one_head, 0)

    def partial_output():
        for block in range(2):

            def one_head(head, carry, block=block):
                item = block * KVH + head
                partial[item] = jnp.dot(
                    softmax[item, :, : 2 * BLOCK], jnp.concatenate(near_pair(1, block, head), axis=0),
                    preferred_element_type=jnp.float32,
                )
                return carry

            lax.fori_loop(0, KVH, one_head, 0)

    def output_task():
        yield plan["output"], []
        for block in range(2):

            def one_head(head, carry, block=block):
                item = block * KVH + head
                result = partial[item] + jnp.dot(
                    softmax[item, :, 2 * BLOCK :], chosen(1, block, head), preferred_element_type=jnp.float32
                )
                result = result.astype(jnp.bfloat16)
                for g in range(GROUP):
                    lanes = pl.ds(pl.multiple_of((head * GROUP + g) * DH, DH), DH)
                    out_ref[block * BLOCK : (block + 1) * BLOCK, lanes] = result[g * BLOCK : (g + 1) * BLOCK]
                return carry

            lax.fori_loop(0, KVH, one_head, 0)

    half = KVH // 2
    both = Group(lambda wake: [output_task()])
    softmax_tasks = [
        both.add(weights_task(block, (begin, begin + half), plan["softmax"][block * 2 + begin // half]))
        for block in range(2) for begin in (0, half)
    ]
    values_ready = both.add(iter(()))
    groups = [
        Group(lambda wake: exchange(0, softmax_tasks)),
        Group(lambda wake: exchange(1, [values_ready])),
    ]
    gathers = [
        [
            gather_weight(place, copies, groups[kind], weights, kind, part, axes, plan["begin"][kind], plan["spans"])
            for part, axes in enumerate((("y", "x"), ("x", "y")))
        ]
        for kind in range(2)
    ]
    tasks = [first_task(0, gathers[0]), list_task(), first_task(1, gathers[1])]
    run_tasks(tasks)
    copies.sent()
    assert len(copies.started) == COPIES, len(copies.started)


PLAN = {
    "first": ((0.1, 2.4), (10.5, 3.0)),
    "lists": ((0.2, 2.4), (14.2, 4.0), 44.5),
    "begin": (10.0, 44.0),
    "spans": (2.0, 5.0, 9.0),
    "exchange": ((43.0, 53.0, 66.0, 79.0, 83.0, 96.5), (74.0, 84.0, 96.0, 107.0, 111.0, 116.0)),
    "softmax": (97.0, 98.0, 99.0, 100.0),
    "output": 117.0,
}


def layer(lists, tokens, queries, key_weight, value_weight, sizes):
    local_tokens, depth = tokens.shape
    part_rows, width = key_weight.shape
    columns, rows = 2 * sizes["y"], sizes["z"]
    hbm = pl.BlockSpec(memory_space=pltpu.HBM)
    kind = Kind.scratch(rows, columns)
    return pl.pallas_call(
        functools.partial(layer_kernel, sizes, PLAN),
        out_shape=jax.ShapeDtypeStruct(queries.shape, jnp.bfloat16),
        in_specs=[hbm] * 5,
        out_specs=pl.BlockSpec(memory_space=pltpu.VMEM),
        scratch_shapes=[
            pltpu.VMEM((2, sizes["x"], rows, sizes["y"], 2 * part_rows, width // 2), jnp.bfloat16),
            pltpu.VMEM((2, local_tokens, depth), jnp.bfloat16),
            pltpu.VMEM(queries.shape, jnp.bfloat16),
            pltpu.VMEM((rows, sizes["y"], 2, 8, LANES), jnp.int32),
            pltpu.VMEM((8, LANES), jnp.int32),
            pltpu.SMEM((8, LANES), jnp.int32),
            pltpu.SMEM((8, LANES), jnp.int32),
            pltpu.VMEM((2 * KVH, GROUP * BLOCK, 3 * BLOCK), jnp.bfloat16),
            pltpu.VMEM((2 * KVH, GROUP * BLOCK, DH), jnp.float32),
            *kind,
            *kind,
            pltpu.SemaphoreType.DMA((8,)),
            pltpu.SemaphoreType.DMA((COPIES,)),
            pltpu.SemaphoreType.DMA((COPIES,)),
        ],
        compiler_params=pltpu.CompilerParams(
            collective_id=0, has_side_effects=True, vmem_limit_bytes=58 << 20
        ),
        name="layer",
    )(lists, tokens, queries, key_weight, value_weight)


COPIES = 180


def local(tokens, queries, key_weight, value_weight, sorted_blocks):
    devices = lax.axis_size("seq")
    sizes = {"x": lax.axis_size("fsdp"), "y": 4, "z": devices // 8}
    own = sorted_blocks[0].T.reshape(-1)
    lists = jnp.broadcast_to(jnp.pad(own, (0, LANES - own.shape[0]), constant_values=-1), (8, LANES))
    return layer(lists, tokens[0], queries[0], key_weight, value_weight, sizes)[None]


def solution(mesh):
    placed = (
        P("fsdp", "seq", None),
        P("fsdp", "seq", None),
        P(("fsdp", "seq"), None),
        P(("fsdp", "seq"), None),
        P("fsdp", None, "seq"),
    )
    return jax.shard_map(
        local, mesh=mesh, in_specs=placed, out_specs=P("fsdp", "seq", None), check_vma=False
    )
```
